32 devices in a mesh: groups: 2 (over x), gx: 16 (over z, y, core).
Axes of the slice: x: 2, y: 2, z: 4, core: 2. Of those that a mesh axis runs over, the one named last changes fastest.
Arguments:
- first_volume: bfloat16 [512, 32, 128], P(('groups', 'gx')), parts along dimension 0, may hold values from -6 to 6
- second_volume: bfloat16 [512, 32, 128], P(('groups', 'gx')), parts along dimension 0, may hold values from -6 to 6
- shift_x: int32 [32, 8], P(('groups', 'gx')), parts along dimension 0, may hold values from -48 to 48
- shift_y: int32 [32, 8], P(('groups', 'gx')), parts along dimension 0, may hold values from -16 to 16
Outputs:
- corrected: float32 [32, 16, 16, 128], P(('groups', 'gx')), parts along dimension 0
The draws below stay inside these ranges and needn't reach their ends.
There are 2 independent parts, one for each index of `groups`. The reference program is written for one: setup_inputs(seed, part) draws one part's arguments, and reference() takes and returns one part's arrays. A program takes and returns all parts, laid end to end along the dimension named above; each array names one. Nothing has to cross between parts.
All inputs are finite; a program needn't handle non-finite values.
Results may differ from the reference program's by a relative error of at most 0.0003.
Values may be sent and summed in bfloat16 or wider, within the bound.
No kernel may reach another device: no remote copies, remote signals or barrier semaphores. Data moves between devices by JAX's collectives and lax.ppermute only.
A program may use at most 64 MiB of HBM per device.

```python
import jax
import jax.numpy as jnp
from jax import lax

WIN = 32
STEP = 16
ZS = 32
SR = 16
REACH = 3
WY = 8
NWX = 16
NX = 256
NY = 128


def plant(result, key, smallest, top_value):
    spot = [jax.random.randint(jax.random.fold_in(key, axis), (), 0, length) for axis, length in enumerate(result.shape)]
    main_axis = result.shape.index(max(result.shape))
    beside = spot[:main_axis] + [(spot[main_axis] + 1) % result.shape[main_axis]] + spot[main_axis + 1:]
    return result.at[tuple(spot)].set(smallest).at[tuple(beside)].set(top_value)


def levels(own_key, extent, split, least, high):
    level = 1.0
    for position, parts in split:
        steps = jax.random.uniform(jax.random.fold_in(jax.random.fold_in(own_key, 6), position), (parts,), jnp.float32, least / len(split), high / len(split))
        level = level * jnp.repeat(jnp.exp(steps), extent[position] // parts).reshape((-1,) + (1,) * (len(extent) - 1 - position))
    return level


def normal_values(own_key, dims, scale, limit, shards=(), kind=jnp.bfloat16):
    loudness = levels(own_key, dims, shards, -0.22, 0.18) if shards else 1.0
    result = jax.random.normal(own_key, dims, jnp.float32) * scale * loudness
    return jnp.minimum(jnp.maximum(result, -limit), limit).astype(kind)


def setup_inputs(seed: int = 0, part: int = 0) -> dict:
    key_of = jax.random.split(jax.random.key(seed), 5)
    part_splits = jax.random.split(jax.random.fold_in(key_of[4], part), 5)
    return {
        "first_volume": normal_values(part_splits[0], (NX, ZS, NY), 1.0, 6.0, ((0, 16),)),
        "second_volume": normal_values(part_splits[1], (NX, ZS, NY), 1.0, 6.0, ((0, 16),)),
        "shift_x": plant(jax.random.randint(part_splits[2], (NWX, WY), -REACH * STEP, REACH * STEP + 1), jax.random.fold_in(part_splits[2], 1), -REACH * STEP, REACH * STEP).astype(jnp.int32),
        "shift_y": plant(jax.random.randint(part_splits[3], (NWX, WY), -STEP, STEP + 1), jax.random.fold_in(part_splits[3], 1), -STEP, STEP).astype(jnp.int32),
    }


def window_maps(first_win, second_win):
    first_win = first_win.astype(jnp.float32)
    second_win = second_win.astype(jnp.float32)
    first_zero = first_win - jnp.mean(first_win)
    second_zero = second_win - jnp.mean(second_win)
    first_scale = jnp.sqrt(jnp.mean(first_zero * first_zero) + 1e-06)
    second_scale = jnp.sqrt(jnp.mean(second_zero * second_zero) + 1e-06)
    spectrum = jnp.conj(jnp.fft.fftn(first_zero)) * jnp.fft.fftn(second_zero)
    correlation = jnp.real(jnp.fft.ifftn(spectrum)).astype(jnp.float32)
    centred = (jnp.arange(SR, dtype=jnp.int32) - SR // 2) % WIN
    cropped = correlation[centred][:, centred][:, :, centred]
    return cropped / (WIN ** 1.5 * first_scale * second_scale)

def reference(first_volume, second_volume, shift_x, shift_y):
    first_padded = jnp.pad(first_volume, ((0, STEP), (0, 0), (0, STEP)))
    second_padded = jnp.pad(second_volume, ((REACH * STEP, (REACH + 1) * STEP), (0, 0), (STEP, 2 * STEP)))
    window_rows = jnp.arange(WY, dtype=jnp.int32)

    def one_column(column):

        def one_window(row, step_x, step_y):
            zero_index = jnp.zeros((), jnp.int32)
            first_win = lax.dynamic_slice(first_padded, (column * STEP, zero_index, row * STEP), (WIN, ZS, WIN))
            second_win = lax.dynamic_slice(second_padded, (column * STEP + step_x + REACH * STEP, zero_index, row * STEP + step_y + STEP), (WIN, ZS, WIN))
            return window_maps(first_win, second_win)
        return jax.vmap(one_window)(window_rows, shift_x[column], shift_y[column])
    peak_maps = lax.map(one_column, jnp.arange(NWX, dtype=jnp.int32))
    ones_column = jnp.ones_like(peak_maps[:1])
    left_maps = jnp.concatenate([ones_column, peak_maps[:-1]], 0)
    right_maps = jnp.concatenate([peak_maps[1:], ones_column], 0)
    ones_row = jnp.ones_like(peak_maps[:, :1])
    below_maps = jnp.concatenate([ones_row, peak_maps[:, :-1]], 1)
    above_maps = jnp.concatenate([peak_maps[:, 1:], ones_row], 1)
    product = peak_maps * left_maps * right_maps * below_maps * above_maps
    return product.transpose(0, 2, 3, 1, 4).reshape(NWX, SR, SR, WY * SR)
```

```python
import math

import jax
import jax.numpy as jnp
import numpy as np
from jax import lax
from jax.experimental import pallas as pl
from jax.experimental.pallas import tpu as pltpu
from jax.sharding import PartitionSpec as P

WIN = 32
STEP = 16
ZS = 32
SR = 16
WY = 8
NY = WY * STEP
LANES = 128
HALF = WIN // 2
BF16 = jnp.bfloat16
F32 = jnp.float32
VMEM_LIMIT = 48 * 2**20

Z_ORDER = np.array([*range(16), 16, *range(31, 16, -1)])


def split_table(table):
    high = np.asarray(table, np.float32).astype(BF16)
    low = (np.asarray(table, np.float64) - high.astype(np.float64)).astype(BF16)
    return high, low


def phase(numbers):
    return 2.0 * math.pi * (np.asarray(numbers) % WIN) / WIN


def y_columns():
    angles = phase(np.outer(np.arange(WIN), np.arange(HALF)))
    real, imag = np.cos(angles), -np.sin(angles)
    imag[:, 0] = 1.0 - 2.0 * (np.arange(WIN) % 2)
    return real, imag


def first_y_table():
    real, imag = y_columns()
    table = np.zeros((NY + STEP, 2, WY, HALF))
    for j in range(WY):
        table[j * STEP : j * STEP + WIN, 0, j] = real
        table[j * STEP : j * STEP + WIN, 1, j] = imag
    high, low = split_table(table[:NY].reshape(NY, 2 * LANES))
    return np.concatenate([high, low], 0)


def second_y_table():
    real, imag = y_columns()
    table = np.zeros((WY, WIN, 2, WY, HALF))
    for j in range(WY):
        table[j, :, 0, j] = real
        table[j, :, 1, j] = imag
    return split_table(table.reshape(2 * LANES, 2 * LANES))


def three_terms(table, axis):
    high, low = split_table(table)
    return np.concatenate([high, high, low], axis)


def z_table():
    angles = phase(np.outer(Z_ORDER, np.arange(ZS)))
    four = np.eye(4)
    cosine, sine = np.kron(four, np.cos(angles)), np.kron(four, np.sin(angles))
    return three_terms(np.block([[cosine, sine], [-sine, cosine]]), 1)


def z_inverse_table():
    angles = phase(np.outer(np.arange(SR) - SR // 2, Z_ORDER))
    four = np.eye(4)
    cosine, sine = np.kron(four, np.cos(angles)), np.kron(four, np.sin(angles))
    return three_terms(np.block([[cosine, -sine], [sine, cosine]]), 1)


def y_inverse_table():
    shifts = np.arange(SR) - SR // 2
    angles = phase(np.outer(np.arange(HALF), shifts))
    real, imag = 2.0 * np.cos(angles), -2.0 * np.sin(angles)
    real[0] = 1.0
    imag[0] = 1.0 - 2.0 * (shifts % 2)
    eight = np.eye(WY)
    table = np.concatenate([np.kron(eight, real), np.kron(eight, imag)], 0)
    return three_terms(table / (WIN * WIN), 0)


def dot(a, b):
    return jnp.dot(a, b, preferred_element_type=F32)


def split(value, axis):
    high = value.astype(BF16)
    low = (value - high.astype(F32)).astype(BF16)
    return jnp.concatenate([high, low, high], axis)


def positions(shape):
    rows = lax.broadcasted_iota(jnp.int32, shape, len(shape) - 2)
    lanes = lax.broadcasted_iota(jnp.int32, shape, len(shape) - 1)
    return rows, lanes % HALF == 0


def z_stage(part_0, part_1, table_ref, real_ref, imag_ref, start):
    columns = [
        jnp.concatenate([part[:, :LANES], part[:, LANES:]], 0) for part in (part_0, part_1)
    ]
    slots = dot(table_ref[...], split(jnp.concatenate(columns, 1), 0))
    rows, zero_lane = positions((4, 8, LANES))
    mixed = [zero_lane & (rows != 0), zero_lane]
    weight = jnp.where(zero_lane & (rows == 0), 1.0, 2.0)
    no_mean = jnp.where(zero_lane & (rows == 0), 0.0, 2.0)
    energy = jnp.zeros((8, LANES), F32)
    for h in range(2):
        lanes = slice(h * LANES, (h + 1) * LANES)
        real = slots[: 4 * ZS, lanes].reshape(4, ZS, LANES)
        imag = slots[4 * ZS :, lanes].reshape(4, ZS, LANES)
        where_x = pl.ds(start + 4 * h, 4)
        for group in range(2):
            up = slice(group * 8, group * 8 + 8)
            down = slice(group * 8 + 16, group * 8 + 24)
            ur, ui, dr, di = real[:, up], imag[:, up], real[:, down], imag[:, down]
            mask = mixed[group]
            new = (
                jnp.where(mask, 0.5 * (ur + dr), ur),
                jnp.where(mask, 0.5 * (ui - di), ui),
                jnp.where(mask, 0.5 * (ui + di), dr),
                jnp.where(mask, 0.5 * (dr - ur), di),
            )
            real_ref[where_x, up] = new[0]
            imag_ref[where_x, up] = new[1]
            real_ref[where_x, down] = new[2]
            imag_ref[where_x, down] = new[3]
            if group == 0:
                parts = no_mean * new[0] * new[0] + weight * (
                    new[1] * new[1] + new[2] * new[2] + new[3] * new[3]
                )
            else:
                parts = 2.0 * sum(v * v for v in new)
            energy = energy + jnp.sum(parts, 0)
    return energy


def finish_stage(energy, real_ref):
    rows, zero_lane = positions((8, LANES))
    is_mean = zero_lane & (rows == 0)
    block = real_ref[:, 0:8]
    means = jnp.where(is_mean, jnp.sum(block, 0) * (1.0 / WIN), 0.0)
    centred = block - means[None]
    real_ref[:, 0:8] = centred
    total = energy + jnp.sum(jnp.where(is_mean[None], centred * centred, 0.0), 0)
    total = jnp.broadcast_to(jnp.sum(total, 0, keepdims=True), (8, LANES))
    group_row = lax.broadcasted_iota(jnp.int32, (LANES, LANES), 0) // HALF
    group_col = lax.broadcasted_iota(jnp.int32, (LANES, LANES), 1) // HALF
    same = (group_row == group_col).astype(F32)
    summed = jnp.dot(total, same, precision=lax.Precision.HIGHEST, preferred_element_type=F32)
    return summed * (1.0 / (ZS * WIN * WIN * ZS * WIN))


def first_kernel(tile_ref, next_ref, y_ref, z_ref, real_ref, imag_ref, var_ref):
    energy = jnp.zeros((8, LANES), F32)
    table = y_ref[...]
    for source, base in ((tile_ref, 0), (next_ref, STEP)):
        for start in range(0, STEP, 8):
            rows = source[start : start + 8].reshape(8 * ZS, NY)
            values = dot(jnp.concatenate([rows, rows], 1), table)
            energy = energy + z_stage(
                values[: 4 * ZS], values[4 * ZS :], z_ref, real_ref, imag_ref, base + start
            )
    var_ref[...] = finish_stage(energy, real_ref)


def second_kernel(
    starts_ref,
    own_ref,
    mate_ref,
    near_ref,
    far_ref,
    mate_near_ref,
    mate_far_ref,
    first_real_ref,
    first_imag_ref,
    first_var_ref,
    y_high_ref,
    y_low_ref,
    z_ref,
    z_inverse_ref,
    y_inverse_ref,
    out_ref,
    region_ref,
    real_ref,
    imag_ref,
    cross_real_ref,
    cross_imag_ref,
    sems,
):
    odd = starts_ref[2, 0]
    two = 2 * STEP
    copies = [
        pltpu.make_async_copy(source, region_ref.at[pl.ds(place, source.shape[0])], sems.at[n])
        for n, (source, place) in enumerate(
            (
                (own_ref, 2 * two + STEP * odd),
                (mate_ref, 2 * two + STEP * (1 - odd)),
                (near_ref, two + 2 * two * (1 - odd)),
                (far_ref, 4 * two * (1 - odd)),
                (mate_near_ref, two + 2 * two * odd),
                (mate_far_ref, 4 * two * odd),
            )
        )
    ]
    for copy in copies:
        copy.start()
    for copy in copies:
        copy.wait()

    lane = lax.broadcasted_iota(jnp.int32, (1, LANES), 1)

    def eight_x(step, energy):
        start = step * 8
        packs = []
        for half in range(2):
            total = None
            for n in range(4):
                j = half * 4 + n
                start_y = starts_ref[1, j]
                block = region_ref[pl.ds(starts_ref[0, j] + start, 8)].reshape(8 * ZS, NY)
                turned = pltpu.roll(block.astype(F32), (n * WIN - start_y) & (LANES - 1), 1)
                y = lane - n * WIN + start_y
                inside = (lane // WIN == n) & (y >= 0) & (y < NY)
                if total is None:
                    total = jnp.where(inside, turned, 0.0)
                else:
                    total = jnp.where(inside, turned, total)
            packs.append(total.astype(BF16))
        windows = jnp.concatenate(packs, 1)
        values = dot(windows, y_high_ref[...]) + dot(windows, y_low_ref[...])
        return energy + z_stage(
            values[: 4 * ZS], values[4 * ZS :], z_ref, real_ref, imag_ref, start
        )

    energy = lax.fori_loop(0, WIN // 8, eight_x, jnp.zeros((8, LANES), F32))
    second_var = finish_stage(energy, real_ref)

    rows, zero_lane = positions((8, LANES))
    special = zero_lane & (rows == 0)

    def eight_slots(block, carry):
        where_z = pl.ds(pl.multiple_of(block * 8, 8), 8)
        alone = special & (block % 2 == 0)
        for base in range(0, SR, 8):
            rr = [None] * 8
            ii = [None] * 8
            ri = [None] * 8
            for x in range(WIN):
                fr = first_real_ref[x, where_z]
                fi = first_imag_ref[x, where_z]
                for s in range(8):
                    at = (x + base + s - SR // 2) % WIN
                    gr = real_ref[at, where_z]
                    gi = imag_ref[at, where_z]
                    if x == 0:
                        rr[s], ii[s], ri[s] = fr * gr, fi * gi, fr * gi - fi * gr
                    else:
                        rr[s] = rr[s] + fr * gr
                        ii[s] = ii[s] + fi * gi
                        ri[s] = ri[s] + fr * gi - fi * gr
            for s in range(8):
                cross_real_ref[base + s, where_z] = jnp.where(alone, rr[s], rr[s] + ii[s])
                cross_imag_ref[base + s, where_z] = jnp.where(alone, ii[s], ri[s])
        return carry

    lax.fori_loop(0, ZS // 8, eight_slots, 0)

    rows, zero_lane = positions((4, 8, LANES))
    mixed = [zero_lane & (rows != 0), zero_lane]
    scale = 1.0 / (
        WIN**1.5 * (jnp.sqrt(first_var_ref[...] + 1e-6) * jnp.sqrt(second_var + 1e-6))
    )
    for start in range(0, SR, 8):
        columns = []
        for quarter in range(start, start + 8, 4):
            where_x = slice(quarter, quarter + 4)
            real = [None] * 4
            imag = [None] * 4
            for group in range(2):
                up = slice(group * 8, group * 8 + 8)
                down = slice(group * 8 + 16, group * 8 + 24)
                ur, ui = cross_real_ref[where_x, up], cross_imag_ref[where_x, up]
                dr, di = cross_real_ref[where_x, down], cross_imag_ref[where_x, down]
                mask = mixed[group]
                real[group] = jnp.where(mask, ur - di, ur)
                imag[group] = jnp.where(mask, ui + dr, ui)
                real[group + 2] = jnp.where(mask, ur + di, dr)
                imag[group + 2] = jnp.where(mask, dr - ui, di)
            columns.append(
                jnp.concatenate(
                    [jnp.concatenate(v, 1).reshape(4 * ZS, LANES) for v in (real, imag)], 0
                )
            )
        slots = dot(z_inverse_ref[...], split(jnp.concatenate(columns, 1), 0))
        for h in range(2):
            lanes = slice(h * LANES, (h + 1) * LANES)
            pair = jnp.concatenate([slots[: 4 * SR, lanes], slots[4 * SR :, lanes]], 1)
            values = dot(split(pair, 1), y_inverse_ref[...])
            where_out = slice((start + 4 * h) * SR, (start + 4 * h + 4) * SR)
            out_ref[where_out] = values * scale[0:1]


def product_kernel(edge_ref, own_ref, mate_ref, other_ref, out_ref):
    own = own_ref[...]
    lane = lax.broadcasted_iota(jnp.int32, own.shape, 1)
    below = jnp.where(lane < SR, 1.0, pltpu.roll(own, SR, 1))
    above = jnp.where(lane >= LANES - SR, 1.0, pltpu.roll(own, LANES - SR, 1))
    other = jnp.where(edge_ref[0] == 1, 1.0, other_ref[...])
    out_ref[...] = own * mate_ref[...] * other * below * above


def params():
    return pltpu.CompilerParams(vmem_limit_bytes=VMEM_LIMIT)


VMEM = pl.BlockSpec(memory_space=pltpu.VMEM)
SMEM = pl.BlockSpec(memory_space=pltpu.SMEM)
ANY = pl.BlockSpec(memory_space=pl.ANY)


def local(first_volume, second_volume, shift_x, shift_y):
    size = lax.axis_size("gx")
    chips = size // 2
    position = lax.axis_index("gx")
    odd = position % 2

    def send(value, pairs):
        return lax.ppermute(value, "gx", pairs)

    mates = [(i, i ^ 1) for i in range(size)]
    near = [(2 * q + 2, 2 * q) for q in range(chips - 1)]
    near += [(2 * q - 1, 2 * q + 1) for q in range(1, chips)]
    far = [(2 * q + 4, 2 * q) for q in range(chips - 2)]
    far += [(2 * q - 3, 2 * q + 1) for q in range(2, chips)]
    after = [(2 * q + 2, 2 * q + 1) for q in range(chips - 1)]
    across = after + [(b, a) for a, b in after]

    mate_tile = send(second_volume, mates)
    low = jnp.where(odd == 0, second_volume, mate_tile)
    high = jnp.where(odd == 0, mate_tile, second_volume)
    pair = jnp.concatenate([low, high], 0)
    far_pair = send(pair, far)
    near_pair = send(pair, near)
    next_tile = send(first_volume, [(i + 1, i) for i in range(size - 1)])
    mate_far = send(far_pair, mates)
    mate_near = send(near_pair, mates)

    spectrum = jax.ShapeDtypeStruct((WIN, ZS, LANES), F32)
    first_real, first_imag, first_var = pl.pallas_call(
        first_kernel,
        out_shape=(spectrum, spectrum, jax.ShapeDtypeStruct((8, LANES), F32)),
        in_specs=[VMEM] * 4,
        out_specs=(VMEM, VMEM, VMEM),
        compiler_params=params(),
        name="first_spectra",
    )(first_volume, next_tile, first_y_table(), z_table())

    starts_x = shift_x[0] + STEP * (4 + odd)
    starts_y = shift_y[0] + jnp.arange(WY, dtype=jnp.int32) * STEP
    starts = jnp.stack([starts_x, starts_y, jnp.full((WY,), odd, jnp.int32)], 0)
    y_high, y_low = second_y_table()
    maps = pl.pallas_call(
        second_kernel,
        out_shape=jax.ShapeDtypeStruct((SR * SR, LANES), F32),
        in_specs=[SMEM] + [ANY] * 6 + [VMEM] * 8,
        out_specs=VMEM,
        scratch_shapes=[
            pltpu.VMEM((10 * STEP, ZS, NY), BF16),
            pltpu.VMEM((WIN, ZS, LANES), F32),
            pltpu.VMEM((WIN, ZS, LANES), F32),
            pltpu.VMEM((SR, ZS, LANES), F32),
            pltpu.VMEM((SR, ZS, LANES), F32),
            pltpu.SemaphoreType.DMA((6,)),
        ],
        compiler_params=params(),
        name="second_maps",
    )(
        starts,
        second_volume,
        mate_tile,
        near_pair,
        far_pair,
        mate_near,
        mate_far,
        first_real,
        first_imag,
        first_var,
        y_high,
        y_low,
        z_table(),
        z_inverse_table(),
        y_inverse_table(),
    )

    other_maps = send(maps, across)
    mate_maps = send(maps, mates)
    edge = ((position == 0) | (position == size - 1)).astype(jnp.int32).reshape(1)
    product = pl.pallas_call(
        product_kernel,
        out_shape=jax.ShapeDtypeStruct((SR * SR, LANES), F32),
        in_specs=[SMEM, VMEM, VMEM, VMEM],
        out_specs=VMEM,
        compiler_params=params(),
        name="product",
    )(edge, maps, mate_maps, other_maps)
    return product.reshape(1, SR, SR, LANES)


def solution(mesh):
    return jax.shard_map(
        local,
        mesh=mesh,
        in_specs=(
            P(("groups", "gx"), None, None),
            P(("groups", "gx"), None, None),
            P(("groups", "gx"), None),
            P(("groups", "gx"), None),
        ),
        out_specs=P(("groups", "gx"), None, None, None),
        check_vma=False,
    )
```

```python
import math

import jax
import jax.numpy as jnp
import numpy as np
from jax import lax
from jax.experimental import pallas as pl
from jax.experimental.pallas import tpu as pltpu
from jax.sharding import PartitionSpec as P

WIN = 32
STEP = 16
ZS = 32
SR = 16
WY = 8
NY = WY * STEP
LANES = 128
HALF = WIN // 2
BF16 = jnp.bfloat16
F32 = jnp.float32
VMEM_LIMIT = 48 * 2**20

Z_ORDER = np.array([*range(16), 16, *range(31, 16, -1)])


def split_table(table):
    high = np.asarray(table, np.float32).astype(BF16)
    low = (np.asarray(table, np.float64) - high.astype(np.float64)).astype(BF16)
    return high, low


def phase(numbers):
    return 2.0 * math.pi * (np.asarray(numbers) % WIN) / WIN


def y_columns():
    angles = phase(np.outer(np.arange(WIN), np.arange(HALF)))
    real, imag = np.cos(angles), -np.sin(angles)
    imag[:, 0] = 1.0 - 2.0 * (np.arange(WIN) % 2)
    return real, imag


def first_y_table():
    real, imag = y_columns()
    table = np.zeros((NY + STEP, 2, WY, HALF))
    for j in range(WY):
        table[j * STEP : j * STEP + WIN, 0, j] = real
        table[j * STEP : j * STEP + WIN, 1, j] = imag
    high, low = split_table(table[:NY].reshape(NY, 2 * LANES))
    return np.concatenate([high, low], 0)


def second_y_table():
    real, imag = y_columns()
    table = np.zeros((WY, WIN, 2, WY, HALF))
    for j in range(WY):
        table[j, :, 0, j] = real
        table[j, :, 1, j] = imag
    return split_table(table.reshape(2 * LANES, 2 * LANES))


def three_terms(table, axis):
    high, low = split_table(table)
    return np.concatenate([high, high, low], axis)


def z_table():
    angles = phase(np.outer(Z_ORDER, np.arange(ZS)))
    four = np.eye(4)
    cosine, sine = np.kron(four, np.cos(angles)), np.kron(four, np.sin(angles))
    return three_terms(np.block([[cosine, sine], [-sine, cosine]]), 1)


def z_inverse_table():
    angles = phase(np.outer(np.arange(SR) - SR // 2, Z_ORDER))
    four = np.eye(4)
    cosine, sine = np.kron(four, np.cos(angles)), np.kron(four, np.sin(angles))
    return three_terms(np.block([[cosine, -sine], [sine, cosine]]), 1)


def y_inverse_table():
    shifts = np.arange(SR) - SR // 2
    angles = phase(np.outer(np.arange(HALF), shifts))
    real, imag = 2.0 * np.cos(angles), -2.0 * np.sin(angles)
    real[0] = 1.0
    imag[0] = 1.0 - 2.0 * (shifts % 2)
    eight = np.eye(WY)
    table = np.concatenate([np.kron(eight, real), np.kron(eight, imag)], 0)
    return three_terms(table / (WIN * WIN), 0)


def dot(a, b):
    return jnp.dot(a, b, preferred_element_type=F32)


def split(value, axis):
    high = value.astype(BF16)
    low = (value - high.astype(F32)).astype(BF16)
    return jnp.concatenate([high, low, high], axis)


def positions(shape):
    rows = lax.broadcasted_iota(jnp.int32, shape, len(shape) - 2)
    lanes = lax.broadcasted_iota(jnp.int32, shape, len(shape) - 1)
    return rows, lanes % HALF == 0


def z_stage(part_0, part_1, table_ref, real_ref, imag_ref, start):
    columns = [
        jnp.concatenate([part[:, :LANES], part[:, LANES:]], 0) for part in (part_0, part_1)
    ]
    slots = dot(table_ref[...], split(jnp.concatenate(columns, 1), 0))
    rows, zero_lane = positions((4, 8, LANES))
    mixed = [zero_lane & (rows != 0), zero_lane]
    weight = jnp.where(zero_lane & (rows == 0), 1.0, 2.0)
    no_mean = jnp.where(zero_lane & (rows == 0), 0.0, 2.0)
    energy = jnp.zeros((8, LANES), F32)
    for h in range(2):
        lanes = slice(h * LANES, (h + 1) * LANES)
        real = slots[: 4 * ZS, lanes].reshape(4, ZS, LANES)
        imag = slots[4 * ZS :, lanes].reshape(4, ZS, LANES)
        where_x = pl.ds(start + 4 * h, 4)
        for group in range(2):
            up = slice(group * 8, group * 8 + 8)
            down = slice(group * 8 + 16, group * 8 + 24)
            ur, ui, dr, di = real[:, up], imag[:, up], real[:, down], imag[:, down]
            mask = mixed[group]
            new = (
                jnp.where(mask, 0.5 * (ur + dr), ur),
                jnp.where(mask, 0.5 * (ui - di), ui),
                jnp.where(mask, 0.5 * (ui + di), dr),
                jnp.where(mask, 0.5 * (dr - ur), di),
            )
            real_ref[where_x, up] = new[0]
            imag_ref[where_x, up] = new[1]
            real_ref[where_x, down] = new[2]
            imag_ref[where_x, down] = new[3]
            if group == 0:
                parts = no_mean * new[0] * new[0] + weight * (
                    new[1] * new[1] + new[2] * new[2] + new[3] * new[3]
                )
            else:
                parts = 2.0 * sum(v * v for v in new)
            energy = energy + jnp.sum(parts, 0)
    return energy


def finish_stage(energy, block):
    rows, zero_lane = positions((8, LANES))
    is_mean = zero_lane & (rows == 0)
    means = jnp.where(is_mean, jnp.sum(block, 0) * (1.0 / WIN), 0.0)
    centred = block - means[None]
    total = energy + jnp.sum(jnp.where(is_mean[None], centred * centred, 0.0), 0)
    total = jnp.broadcast_to(jnp.sum(total, 0, keepdims=True), (8, LANES))
    group_row = lax.broadcasted_iota(jnp.int32, (LANES, LANES), 0) // HALF
    group_col = lax.broadcasted_iota(jnp.int32, (LANES, LANES), 1) // HALF
    same = (group_row == group_col).astype(F32)
    summed = jnp.dot(total, same, precision=lax.Precision.HIGHEST, preferred_element_type=F32)
    return centred, summed * (1.0 / (ZS * WIN * WIN * ZS * WIN))


def first_kernel(use_ref, tile_ref, other_ref, y_ref, z_ref, real_ref, imag_ref, energy_ref):
    energy = jnp.zeros((8, LANES), F32)
    table = y_ref[...]
    use = use_ref[0].astype(BF16)
    use_other = use_ref[1].astype(BF16)
    for start in range(0, STEP, 8):
        rows = tile_ref[start : start + 8] * use + other_ref[start : start + 8] * use_other
        rows = rows.reshape(8 * ZS, NY)
        values = dot(jnp.concatenate([rows, rows], 1), table)
        energy = energy + z_stage(
            values[: 4 * ZS], values[4 * ZS :], z_ref, real_ref, imag_ref, start
        )
    energy_ref[...] = energy


def second_kernel(
    starts_ref,
    own_ref,
    mate_ref,
    near_ref,
    far_ref,
    mate_near_ref,
    mate_far_ref,
    low_real_ref,
    low_imag_ref,
    low_energy_ref,
    high_real_ref,
    high_imag_ref,
    high_energy_ref,
    y_high_ref,
    y_low_ref,
    z_ref,
    z_inverse_ref,
    y_inverse_ref,
    out_ref,
    region_ref,
    real_ref,
    imag_ref,
    cross_real_ref,
    cross_imag_ref,
    sems,
):
    odd = starts_ref[2, 0]
    tiles_below = starts_ref[2, 1]
    tiles = starts_ref[2, 2]
    two = 2 * STEP
    copies = [
        pltpu.make_async_copy(source, region_ref.at[pl.ds(place, source.shape[0])], sems.at[n])
        for n, (source, place) in enumerate(
            (
                (own_ref, 2 * two + STEP * odd),
                (mate_ref, 2 * two + STEP * (1 - odd)),
                (near_ref, two + 2 * two * (1 - odd)),
                (far_ref, 4 * two * (1 - odd)),
                (mate_near_ref, two + 2 * two * odd),
                (mate_far_ref, 4 * two * odd),
            )
        )
    ]
    for copy in copies:
        copy.start()
    for copy in copies:
        copy.wait()
    for tile in range(10):

        @pl.when((tiles_below + tile < 0) | (tiles_below + tile >= tiles))
        def _(tile=tile):
            region_ref[tile * STEP : (tile + 1) * STEP] = jnp.zeros((STEP, ZS, NY), BF16)

    lane = lax.broadcasted_iota(jnp.int32, (1, LANES), 1)

    def eight_x(step, energy):
        start = step * 8
        packs = []
        for half in range(2):
            total = None
            for n in range(4):
                j = half * 4 + n
                start_y = starts_ref[1, j]
                block = region_ref[pl.ds(starts_ref[0, j] + start, 8)].reshape(8 * ZS, NY)
                turned = pltpu.roll(block.astype(F32), (n * WIN - start_y) & (LANES - 1), 1)
                y = lane - n * WIN + start_y
                inside = (lane // WIN == n) & (y >= 0) & (y < NY)
                if total is None:
                    total = jnp.where(inside, turned, 0.0)
                else:
                    total = jnp.where(inside, turned, total)
            packs.append(total.astype(BF16))
        windows = jnp.concatenate(packs, 1)
        values = dot(windows, y_high_ref[...]) + dot(windows, y_low_ref[...])
        return energy + z_stage(
            values[: 4 * ZS], values[4 * ZS :], z_ref, real_ref, imag_ref, start
        )

    energy = lax.fori_loop(0, WIN // 8, eight_x, jnp.zeros((8, LANES), F32))
    real_ref[:, 0:8], second_var = finish_stage(energy, real_ref[:, 0:8])
    first_means = jnp.concatenate([low_real_ref[:, 0:8], high_real_ref[:, 0:8]], 0)
    _, first_var = finish_stage(low_energy_ref[...] + high_energy_ref[...], first_means)

    rows, zero_lane = positions((8, LANES))
    special = zero_lane & (rows == 0)

    def eight_slots(block, carry):
        where_z = pl.ds(pl.multiple_of(block * 8, 8), 8)
        alone = special & (block % 2 == 0)
        for base in range(0, SR, 8):
            rr = [None] * 8
            ii = [None] * 8
            ri = [None] * 8
            for x in range(WIN):
                fr_ref = low_real_ref if x < STEP else high_real_ref
                fi_ref = low_imag_ref if x < STEP else high_imag_ref
                fr = fr_ref[x % STEP, where_z]
                fi = fi_ref[x % STEP, where_z]
                for s in range(8):
                    at = (x + base + s - SR // 2) % WIN
                    gr = real_ref[at, where_z]
                    gi = imag_ref[at, where_z]
                    if x == 0:
                        rr[s], ii[s], ri[s] = fr * gr, fi * gi, fr * gi - fi * gr
                    else:
                        rr[s] = rr[s] + fr * gr
                        ii[s] = ii[s] + fi * gi
                        ri[s] = ri[s] + fr * gi - fi * gr
            for s in range(8):
                cross_real_ref[base + s, where_z] = jnp.where(alone, rr[s], rr[s] + ii[s])
                cross_imag_ref[base + s, where_z] = jnp.where(alone, ii[s], ri[s])
        return carry

    lax.fori_loop(0, ZS // 8, eight_slots, 0)

    rows, zero_lane = positions((4, 8, LANES))
    mixed = [zero_lane & (rows != 0), zero_lane]
    scale = 1.0 / (
        WIN**1.5 * (jnp.sqrt(first_var + 1e-6) * jnp.sqrt(second_var + 1e-6))
    )
    for start in range(0, SR, 8):
        columns = []
        for quarter in range(start, start + 8, 4):
            where_x = slice(quarter, quarter + 4)
            real = [None] * 4
            imag = [None] * 4
            for group in range(2):
                up = slice(group * 8, group * 8 + 8)
                down = slice(group * 8 + 16, group * 8 + 24)
                ur, ui = cross_real_ref[where_x, up], cross_imag_ref[where_x, up]
                dr, di = cross_real_ref[where_x, down], cross_imag_ref[where_x, down]
                mask = mixed[group]
                real[group] = jnp.where(mask, ur - di, ur)
                imag[group] = jnp.where(mask, ui + dr, ui)
                real[group + 2] = jnp.where(mask, ur + di, dr)
                imag[group + 2] = jnp.where(mask, dr - ui, di)
            columns.append(
                jnp.concatenate(
                    [jnp.concatenate(v, 1).reshape(4 * ZS, LANES) for v in (real, imag)], 0
                )
            )
        slots = dot(z_inverse_ref[...], split(jnp.concatenate(columns, 1), 0))
        for h in range(2):
            lanes = slice(h * LANES, (h + 1) * LANES)
            pair = jnp.concatenate([slots[: 4 * SR, lanes], slots[4 * SR :, lanes]], 1)
            values = dot(split(pair, 1), y_inverse_ref[...])
            where_out = slice((start + 4 * h) * SR, (start + 4 * h + 4) * SR)
            out_ref[where_out] = values * scale[0:1]


def product_kernel(edge_ref, own_ref, mate_ref, other_ref, out_ref):
    own = own_ref[...]
    lane = lax.broadcasted_iota(jnp.int32, own.shape, 1)
    below = jnp.where(lane < SR, 1.0, pltpu.roll(own, SR, 1))
    above = jnp.where(lane >= LANES - SR, 1.0, pltpu.roll(own, LANES - SR, 1))
    other = jnp.where(edge_ref[0] == 1, 1.0, other_ref[...])
    out_ref[...] = own * mate_ref[...] * other * below * above


def params():
    return pltpu.CompilerParams(vmem_limit_bytes=VMEM_LIMIT)


VMEM = pl.BlockSpec(memory_space=pltpu.VMEM)
SMEM = pl.BlockSpec(memory_space=pltpu.SMEM)
ANY = pl.BlockSpec(memory_space=pl.ANY)


def local(first_volume, second_volume, shift_x, shift_y):
    size = lax.axis_size("gx")
    chips = size // 2
    position = lax.axis_index("gx")
    odd = position % 2

    def send(value, pairs):
        return lax.ppermute(value, "gx", pairs)

    last = size - 1
    mates = [(i, i ^ 1) for i in range(size)]
    near = [(2 * q + 2, 2 * q) for q in range(chips - 1)] + [(last, last - 1)]
    near += [(2 * q - 1, 2 * q + 1) for q in range(1, chips)] + [(0, 1)]
    far = [(2 * q + 4, 2 * q) for q in range(chips - 2)] + [(last, last - 1), (last - 2, last - 3)]
    far += [(2 * q - 3, 2 * q + 1) for q in range(2, chips)] + [(0, 1), (2, 3)]
    across = [(i, i + 1 if i % 2 else i - 1) for i in range(1, last)] + [(0, 0), (last, last)]

    mate_tile = send(second_volume, mates)
    low = jnp.where(odd == 0, second_volume, mate_tile)
    high = jnp.where(odd == 0, mate_tile, second_volume)
    pair = jnp.concatenate([low, high], 0)
    low_tile, pair = lax.optimization_barrier((first_volume, pair))
    near_pair = send(pair, near)
    far_pair = send(pair, far)
    near_first = send(first_volume, near)
    mate_first = send(first_volume, mates)
    mate_near_first = send(near_first, mates)

    def first_spectra(use, tile, other_tile):
        spectrum = jax.ShapeDtypeStruct((STEP, ZS, LANES), F32)
        return pl.pallas_call(
            first_kernel,
            out_shape=(spectrum, spectrum, jax.ShapeDtypeStruct((8, LANES), F32)),
            in_specs=[SMEM] + [VMEM] * 4,
            out_specs=(VMEM, VMEM, VMEM),
            compiler_params=params(),
            cost_estimate=pl.CostEstimate(
                flops=2 * 10**9, transcendentals=0, bytes_accessed=2 * 10**6
            ),
            name="first_spectra",
        )(use, tile, other_tile, first_y_table(), z_table())

    low_part = first_spectra(jnp.array([1, 0], jnp.int32), low_tile, low_tile)
    far_pair, *low_part = lax.optimization_barrier((far_pair, *low_part))
    mate_far = send(far_pair, mates)
    mate_near = send(near_pair, mates)
    high_use = jnp.stack([(odd == 0) & (position < last), (odd == 1) & (position < last)])
    high_part = first_spectra(high_use.astype(jnp.int32), mate_first, mate_near_first)

    starts_x = shift_x[0] + STEP * (4 + odd)
    starts_y = shift_y[0] + jnp.arange(WY, dtype=jnp.int32) * STEP
    settings = jnp.stack([odd, position - odd - 4, size])
    starts = jnp.stack([starts_x, starts_y, jnp.pad(settings, (0, WY - 3))], 0)
    y_high, y_low = second_y_table()
    maps = pl.pallas_call(
        second_kernel,
        out_shape=jax.ShapeDtypeStruct((SR * SR, LANES), F32),
        in_specs=[SMEM] + [ANY] * 6 + [VMEM] * 11,
        out_specs=VMEM,
        scratch_shapes=[
            pltpu.VMEM((10 * STEP, ZS, NY), BF16),
            pltpu.VMEM((WIN, ZS, LANES), F32),
            pltpu.VMEM((WIN, ZS, LANES), F32),
            pltpu.VMEM((SR, ZS, LANES), F32),
            pltpu.VMEM((SR, ZS, LANES), F32),
            pltpu.SemaphoreType.DMA((6,)),
        ],
        compiler_params=params(),
        name="second_maps",
    )(
        starts,
        second_volume,
        mate_tile,
        near_pair,
        far_pair,
        mate_near,
        mate_far,
        *low_part,
        *high_part,
        y_high,
        y_low,
        z_table(),
        z_inverse_table(),
        y_inverse_table(),
    )

    other_maps = send(maps, across)
    mate_maps = send(maps, mates)
    edge = ((position == 0) | (position == size - 1)).astype(jnp.int32).reshape(1)
    product = pl.pallas_call(
        product_kernel,
        out_shape=jax.ShapeDtypeStruct((SR * SR, LANES), F32),
        in_specs=[SMEM, VMEM, VMEM, VMEM],
        out_specs=VMEM,
        compiler_params=params(),
        name="product",
    )(edge, maps, mate_maps, other_maps)
    return product.reshape(1, SR, SR, LANES)


def solution(mesh):
    return jax.shard_map(
        local,
        mesh=mesh,
        in_specs=(
            P(("groups", "gx"), None, None),
            P(("groups", "gx"), None, None),
            P(("groups", "gx"), None),
            P(("groups", "gx"), None),
        ),
        out_specs=P(("groups", "gx"), None, None, None),
        check_vma=False,
    )
```

```python
import math

import jax
import jax.numpy as jnp
import numpy as np
from jax import lax
from jax.experimental import pallas as pl
from jax.experimental.pallas import tpu as pltpu
from jax.sharding import PartitionSpec as P

WIN = 32
STEP = 16
ZS = 32
SR = 16
WY = 8
NY = WY * STEP
LANES = 128
HALF = WIN // 2
BF16 = jnp.bfloat16
F32 = jnp.float32
VMEM_LIMIT = 48 * 2**20

Z_ORDER = np.array([*range(16), 16, *range(31, 16, -1)])


def split_table(table):
    high = np.asarray(table, np.float32).astype(BF16)
    low = (np.asarray(table, np.float64) - high.astype(np.float64)).astype(BF16)
    return high, low


def phase(numbers):
    return 2.0 * math.pi * (np.asarray(numbers) % WIN) / WIN


def y_columns():
    angles = phase(np.outer(np.arange(WIN), np.arange(HALF)))
    real, imag = np.cos(angles), -np.sin(angles)
    imag[:, 0] = 1.0 - 2.0 * (np.arange(WIN) % 2)
    return real, imag


def first_y_table():
    real, imag = y_columns()
    table = np.zeros((NY + STEP, 2, WY, HALF))
    for j in range(WY):
        table[j * STEP : j * STEP + WIN, 0, j] = real
        table[j * STEP : j * STEP + WIN, 1, j] = imag
    high, low = split_table(table[:NY].reshape(NY, 2 * LANES))
    return np.concatenate([high, low], 0)


def second_y_table():
    real, imag = y_columns()
    table = np.zeros((WY, WIN, 2, WY, HALF))
    for j in range(WY):
        table[j, :, 0, j] = real
        table[j, :, 1, j] = imag
    return split_table(table.reshape(2 * LANES, 2 * LANES))


def three_terms(table, axis):
    high, low = split_table(table)
    return np.concatenate([high, high, low], axis)


def z_table():
    angles = phase(np.outer(Z_ORDER, np.arange(ZS)))
    four = np.eye(4)
    cosine, sine = np.kron(four, np.cos(angles)), np.kron(four, np.sin(angles))
    return three_terms(np.block([[cosine, sine], [-sine, cosine]]), 1)


def z_inverse_table():
    angles = phase(np.outer(np.arange(SR) - SR // 2, Z_ORDER))
    four = np.eye(4)
    cosine, sine = np.kron(four, np.cos(angles)), np.kron(four, np.sin(angles))
    return three_terms(np.block([[cosine, -sine], [sine, cosine]]), 1)


def y_inverse_table():
    shifts = np.arange(SR) - SR // 2
    angles = phase(np.outer(np.arange(HALF), shifts))
    real, imag = 2.0 * np.cos(angles), -2.0 * np.sin(angles)
    real[0] = 1.0
    imag[0] = 1.0 - 2.0 * (shifts % 2)
    eight = np.eye(WY)
    table = np.concatenate([np.kron(eight, real), np.kron(eight, imag)], 0)
    return three_terms(table / (WIN * WIN), 0)


def dot(a, b):
    return jnp.dot(a, b, preferred_element_type=F32)


def split(value, axis):
    high = value.astype(BF16)
    low = (value - high.astype(F32)).astype(BF16)
    return jnp.concatenate([high, low, high], axis)


def positions(shape):
    rows = lax.broadcasted_iota(jnp.int32, shape, len(shape) - 2)
    lanes = lax.broadcasted_iota(jnp.int32, shape, len(shape) - 1)
    return rows, lanes % HALF == 0


def z_stage(part_0, part_1, table_ref, real_ref, imag_ref, start):
    columns = [
        jnp.concatenate([part[:, :LANES], part[:, LANES:]], 0) for part in (part_0, part_1)
    ]
    slots = dot(table_ref[...], split(jnp.concatenate(columns, 1), 0))
    rows, zero_lane = positions((4, 8, LANES))
    mixed = [zero_lane & (rows != 0), zero_lane]
    weight = jnp.where(zero_lane & (rows == 0), 1.0, 2.0)
    no_mean = jnp.where(zero_lane & (rows == 0), 0.0, 2.0)
    energy = jnp.zeros((8, LANES), F32)
    for h in range(2):
        lanes = slice(h * LANES, (h + 1) * LANES)
        real = slots[: 4 * ZS, lanes].reshape(4, ZS, LANES)
        imag = slots[4 * ZS :, lanes].reshape(4, ZS, LANES)
        where_x = pl.ds(start + 4 * h, 4)
        for group in range(2):
            up = slice(group * 8, group * 8 + 8)
            down = slice(group * 8 + 16, group * 8 + 24)
            ur, ui, dr, di = real[:, up], imag[:, up], real[:, down], imag[:, down]
            mask = mixed[group]
            new = (
                jnp.where(mask, 0.5 * (ur + dr), ur),
                jnp.where(mask, 0.5 * (ui - di), ui),
                jnp.where(mask, 0.5 * (ui + di), dr),
                jnp.where(mask, 0.5 * (dr - ur), di),
            )
            real_ref[where_x, up] = new[0]
            imag_ref[where_x, up] = new[1]
            real_ref[where_x, down] = new[2]
            imag_ref[where_x, down] = new[3]
            if group == 0:
                parts = no_mean * new[0] * new[0] + weight * (
                    new[1] * new[1] + new[2] * new[2] + new[3] * new[3]
                )
            else:
                parts = 2.0 * sum(v * v for v in new)
            energy = energy + jnp.sum(parts, 0)
    return energy


def finish_stage(energy, block):
    rows, zero_lane = positions((8, LANES))
    is_mean = zero_lane & (rows == 0)
    means = jnp.where(is_mean, jnp.sum(block, 0) * (1.0 / WIN), 0.0)
    centred = block - means[None]
    total = energy + jnp.sum(jnp.where(is_mean[None], centred * centred, 0.0), 0)
    total = jnp.broadcast_to(jnp.sum(total, 0, keepdims=True), (8, LANES))
    group_row = lax.broadcasted_iota(jnp.int32, (LANES, LANES), 0) // HALF
    group_col = lax.broadcasted_iota(jnp.int32, (LANES, LANES), 1) // HALF
    same = (group_row == group_col).astype(F32)
    summed = jnp.dot(total, same, precision=lax.Precision.HIGHEST, preferred_element_type=F32)
    return centred, summed * (1.0 / (ZS * WIN * WIN * ZS * WIN))


def first_stage(tile, y_ref, z_ref, real_ref, imag_ref, energy_ref):
    energy = jnp.zeros((8, LANES), F32)
    table = y_ref[...]
    for start in range(0, STEP, 8):
        rows = tile[start : start + 8].reshape(8 * ZS, NY)
        values = dot(jnp.concatenate([rows, rows], 1), table)
        energy = energy + z_stage(
            values[: 4 * ZS], values[4 * ZS :], z_ref, real_ref, imag_ref, start
        )
    energy_ref[...] = energy


def low_kernel(tile_hbm, y_hbm, z_hbm, shift_x_hbm, shift_y_hbm, *refs):
    *outs, shift_x_ref, shift_y_ref, tile_ref, y_ref, z_ref, sems = refs
    copies = [
        pltpu.make_async_copy(source, target, sems.at[n])
        for n, (source, target) in enumerate(
            (
                (z_hbm, z_ref),
                (y_hbm, y_ref),
                (tile_hbm, tile_ref),
                (shift_x_hbm, shift_x_ref),
                (shift_y_hbm, shift_y_ref),
            )
        )
    ]
    for copy in copies:
        copy.start()
    for copy in copies:
        copy.wait()
    first_stage(tile_ref[...], y_ref, z_ref, *outs)


def high_kernel(even_ref, odd_ref, *refs):
    position = lax.axis_index("gx")
    inside = position < lax.axis_size("gx") - 1
    odd = position % 2
    use_even = jnp.where(inside & (odd == 0), 1.0, 0.0).astype(BF16)
    use_odd = jnp.where(inside & (odd == 1), 1.0, 0.0).astype(BF16)
    first_stage(even_ref[...] * use_even + odd_ref[...] * use_odd, *refs)


def second_kernel(
    shift_x_ref,
    shift_y_ref,
    own_ref,
    mate_ref,
    near_own_ref,
    near_mate_ref,
    far_own_ref,
    far_mate_ref,
    mate_near_own_ref,
    mate_near_mate_ref,
    mate_far_own_ref,
    mate_far_mate_ref,
    low_real_ref,
    low_imag_ref,
    low_energy_ref,
    high_real_ref,
    high_imag_ref,
    high_energy_ref,
    y_high_ref,
    y_low_ref,
    z_ref,
    z_inverse_ref,
    y_inverse_ref,
    out_ref,
    region_ref,
    real_ref,
    imag_ref,
    cross_real_ref,
    cross_imag_ref,
):
    position = lax.axis_index("gx")
    tiles = lax.axis_size("gx")
    odd = position % 2
    even = 1 - odd
    tiles_below = position - odd - 4
    shifts_x, shifts_y = shift_x_ref[...], shift_y_ref[...]
    starts_x = [shifts_x[0, j] + STEP * (4 + odd) for j in range(WY)]
    starts_y = [shifts_y[0, j] + STEP * j for j in range(WY)]
    tiles_at = (
        (own_ref, 4 + odd),
        (mate_ref, 4 + even),
        (near_own_ref, 3 + 3 * even),
        (near_mate_ref, 2 + 5 * even),
        (far_own_ref, 1 + 7 * even),
        (far_mate_ref, 9 * even),
        (mate_near_own_ref, 3 + 3 * odd),
        (mate_near_mate_ref, 2 + 5 * odd),
        (mate_far_own_ref, 1 + 7 * odd),
        (mate_far_mate_ref, 9 * odd),
    )
    for tile_ref, at in tiles_at:
        region_ref[pl.ds(at * STEP, STEP)] = tile_ref[...]
    for tile in range(10):

        @pl.when((tiles_below + tile < 0) | (tiles_below + tile >= tiles))
        def _(tile=tile):
            region_ref[tile * STEP : (tile + 1) * STEP] = jnp.zeros((STEP, ZS, NY), BF16)

    lane = lax.broadcasted_iota(jnp.int32, (1, LANES), 1)

    def eight_x(step, energy):
        start = step * 8
        packs = []
        for half in range(2):
            total = None
            for n in range(4):
                j = half * 4 + n
                start_y = starts_y[j]
                block = region_ref[pl.ds(starts_x[j] + start, 8)].reshape(8 * ZS, NY)
                turned = pltpu.roll(block.astype(F32), (n * WIN - start_y) & (LANES - 1), 1)
                y = lane - n * WIN + start_y
                inside = (lane // WIN == n) & (y >= 0) & (y < NY)
                if total is None:
                    total = jnp.where(inside, turned, 0.0)
                else:
                    total = jnp.where(inside, turned, total)
            packs.append(total.astype(BF16))
        windows = jnp.concatenate(packs, 1)
        values = dot(windows, y_high_ref[...]) + dot(windows, y_low_ref[...])
        return energy + z_stage(
            values[: 4 * ZS], values[4 * ZS :], z_ref, real_ref, imag_ref, start
        )

    energy = lax.fori_loop(0, WIN // 8, eight_x, jnp.zeros((8, LANES), F32))
    real_ref[:, 0:8], second_var = finish_stage(energy, real_ref[:, 0:8])
    first_means = jnp.concatenate([low_real_ref[:, 0:8], high_real_ref[:, 0:8]], 0)
    _, first_var = finish_stage(low_energy_ref[...] + high_energy_ref[...], first_means)

    rows, zero_lane = positions((8, LANES))
    special = zero_lane & (rows == 0)

    def eight_slots(block, carry):
        where_z = pl.ds(pl.multiple_of(block * 8, 8), 8)
        alone = special & (block % 2 == 0)
        for base in range(0, SR, 8):
            rr = [None] * 8
            ii = [None] * 8
            ri = [None] * 8
            for x in range(WIN):
                fr_ref = low_real_ref if x < STEP else high_real_ref
                fi_ref = low_imag_ref if x < STEP else high_imag_ref
                fr = fr_ref[x % STEP, where_z]
                fi = fi_ref[x % STEP, where_z]
                for s in range(8):
                    at = (x + base + s - SR // 2) % WIN
                    gr = real_ref[at, where_z]
                    gi = imag_ref[at, where_z]
                    if x == 0:
                        rr[s], ii[s], ri[s] = fr * gr, fi * gi, fr * gi - fi * gr
                    else:
                        rr[s] = rr[s] + fr * gr
                        ii[s] = ii[s] + fi * gi
                        ri[s] = ri[s] + fr * gi - fi * gr
            for s in range(8):
                cross_real_ref[base + s, where_z] = jnp.where(alone, rr[s], rr[s] + ii[s])
                cross_imag_ref[base + s, where_z] = jnp.where(alone, ii[s], ri[s])
        return carry

    lax.fori_loop(0, ZS // 8, eight_slots, 0)

    rows, zero_lane = positions((4, 8, LANES))
    mixed = [zero_lane & (rows != 0), zero_lane]
    scale = 1.0 / (
        WIN**1.5 * (jnp.sqrt(first_var + 1e-6) * jnp.sqrt(second_var + 1e-6))
    )
    for start in range(0, SR, 8):
        columns = []
        for quarter in range(start, start + 8, 4):
            where_x = slice(quarter, quarter + 4)
            real = [None] * 4
            imag = [None] * 4
            for group in range(2):
                up = slice(group * 8, group * 8 + 8)
                down = slice(group * 8 + 16, group * 8 + 24)
                ur, ui = cross_real_ref[where_x, up], cross_imag_ref[where_x, up]
                dr, di = cross_real_ref[where_x, down], cross_imag_ref[where_x, down]
                mask = mixed[group]
                real[group] = jnp.where(mask, ur - di, ur)
                imag[group] = jnp.where(mask, ui + dr, ui)
                real[group + 2] = jnp.where(mask, ur + di, dr)
                imag[group + 2] = jnp.where(mask, dr - ui, di)
            columns.append(
                jnp.concatenate(
                    [jnp.concatenate(v, 1).reshape(4 * ZS, LANES) for v in (real, imag)], 0
                )
            )
        slots = dot(z_inverse_ref[...], split(jnp.concatenate(columns, 1), 0))
        for h in range(2):
            lanes = slice(h * LANES, (h + 1) * LANES)
            pair = jnp.concatenate([slots[: 4 * SR, lanes], slots[4 * SR :, lanes]], 1)
            values = dot(split(pair, 1), y_inverse_ref[...])
            where_out = slice((start + 4 * h) * SR, (start + 4 * h + 4) * SR)
            out_ref[where_out] = values * scale[0:1]


def product_kernel(own_ref, mate_ref, other_ref, out_ref):
    position = lax.axis_index("gx")
    edge = (position == 0) | (position == lax.axis_size("gx") - 1)
    own = own_ref[...]
    lane = lax.broadcasted_iota(jnp.int32, own.shape, 1)
    below = jnp.where(lane < SR, 1.0, pltpu.roll(own, SR, 1))
    above = jnp.where(lane >= LANES - SR, 1.0, pltpu.roll(own, LANES - SR, 1))
    other = jnp.where(edge, 1.0, other_ref[...])
    out_ref[...] = own * mate_ref[...] * other * below * above


def params():
    return pltpu.CompilerParams(vmem_limit_bytes=VMEM_LIMIT)


VMEM = pl.BlockSpec(memory_space=pltpu.VMEM)
HBM = pl.BlockSpec(memory_space=pltpu.HBM)


def local(first_volume, second_volume, shift_x, shift_y):
    size = lax.axis_size("gx")
    chips = size // 2

    def send(value, pairs):
        return lax.ppermute(value, "gx", pairs)

    last = size - 1
    mates = [(i, i ^ 1) for i in range(size)]
    near = [(2 * q + 2, 2 * q) for q in range(chips - 1)] + [(last, last - 1)]
    near += [(2 * q - 1, 2 * q + 1) for q in range(1, chips)] + [(0, 1)]
    far = [(2 * q + 4, 2 * q) for q in range(chips - 2)] + [(last, last - 1), (last - 2, last - 3)]
    far += [(2 * q - 3, 2 * q + 1) for q in range(2, chips)] + [(0, 1), (2, 3)]
    across = [(i, i + 1 if i % 2 else i - 1) for i in range(1, last)] + [(0, 0), (last, last)]

    near_first = send(first_volume, near)
    near_own = send(second_volume, near)
    mate_tile = send(second_volume, mates)
    low_tile, mate_tile = lax.optimization_barrier((first_volume, mate_tile))
    near_mate = send(mate_tile, near)
    far_own = send(second_volume, far)
    far_mate = send(mate_tile, far)
    mate_first = send(first_volume, mates)

    tables = (first_y_table(), z_table())
    spectrum = jax.ShapeDtypeStruct((STEP, ZS, LANES), F32)

    def first_spectra(kernel, specs, scratch, more_out, *operands):
        outs = (spectrum, spectrum, jax.ShapeDtypeStruct((8, LANES), F32), *more_out)
        return pl.pallas_call(
            kernel,
            out_shape=outs,
            in_specs=specs,
            out_specs=(VMEM,) * len(outs),
            scratch_shapes=scratch,
            compiler_params=params(),
            cost_estimate=pl.CostEstimate(
                flops=2 * 10**9, transcendentals=0, bytes_accessed=2 * 10**6
            ),
            name="first_spectra",
        )(*operands)

    scratch = [pltpu.VMEM(v.shape, BF16) for v in (first_volume, *tables)]
    scratch.append(pltpu.SemaphoreType.DMA((5,)))
    in_hbm = [
        pltpu.with_memory_space_constraint(jnp.asarray(v), pltpu.HBM)
        for v in (low_tile, *tables, shift_x, shift_y)
    ]
    shifts = [jax.ShapeDtypeStruct(v.shape, v.dtype) for v in (shift_x, shift_y)]
    *low_part, shift_x, shift_y = first_spectra(low_kernel, [HBM] * 5, scratch, shifts, *in_hbm)
    near_first, *low_part = lax.optimization_barrier((near_first, *low_part))
    mate_near_first = send(near_first, mates)
    side = (near_own, near_mate, far_own, far_mate)
    mate_side = [send(tile, mates) for tile in side]
    high_part = first_spectra(high_kernel, [VMEM] * 4, [], [], mate_first, mate_near_first, *tables)

    y_high, y_low = second_y_table()
    maps = pl.pallas_call(
        second_kernel,
        out_shape=jax.ShapeDtypeStruct((SR * SR, LANES), F32),
        in_specs=[VMEM] * 23,
        out_specs=VMEM,
        scratch_shapes=[
            pltpu.VMEM((10 * STEP, ZS, NY), BF16),
            pltpu.VMEM((WIN, ZS, LANES), F32),
            pltpu.VMEM((WIN, ZS, LANES), F32),
            pltpu.VMEM((SR, ZS, LANES), F32),
            pltpu.VMEM((SR, ZS, LANES), F32),
        ],
        compiler_params=params(),
        name="second_maps",
    )(
        shift_x,
        shift_y,
        second_volume,
        mate_tile,
        *side,
        *mate_side,
        *low_part,
        *high_part,
        y_high,
        y_low,
        z_table(),
        z_inverse_table(),
        y_inverse_table(),
    )

    other_maps = send(maps, across)
    mate_maps = send(maps, mates)
    product = pl.pallas_call(
        product_kernel,
        out_shape=jax.ShapeDtypeStruct((SR * SR, LANES), F32),
        in_specs=[VMEM] * 3,
        out_specs=VMEM,
        compiler_params=params(),
        name="product",
    )(maps, mate_maps, other_maps)
    return product.reshape(1, SR, SR, LANES)


def solution(mesh):
    return jax.shard_map(
        local,
        mesh=mesh,
        in_specs=(
            P(("groups", "gx"), None, None),
            P(("groups", "gx"), None, None),
            P(("groups", "gx"), None),
            P(("groups", "gx"), None),
        ),
        out_specs=P(("groups", "gx"), None, None, None),
        check_vma=False,
    )
```

```python
import math

import jax
import jax.numpy as jnp
import numpy as np
from jax import lax
from jax.experimental import pallas as pl
from jax.experimental.pallas import tpu as pltpu
from jax.sharding import PartitionSpec as P

WIN = 32
STEP = 16
ZS = 32
SR = 16
WY = 8
NY = WY * STEP
LANES = 128
HALF = WIN // 2
BF16 = jnp.bfloat16
F32 = jnp.float32
VMEM_LIMIT = 48 * 2**20

Z_ORDER = np.array([*range(16), 16, *range(31, 16, -1)])


def split_table(table):
    high = np.asarray(table, np.float32).astype(BF16)
    low = (np.asarray(table, np.float64) - high.astype(np.float64)).astype(BF16)
    return high, low


def phase(numbers):
    return 2.0 * math.pi * (np.asarray(numbers) % WIN) / WIN


def y_columns():
    angles = phase(np.outer(np.arange(WIN), np.arange(HALF)))
    real, imag = np.cos(angles), -np.sin(angles)
    imag[:, 0] = 1.0 - 2.0 * (np.arange(WIN) % 2)
    return real, imag


def second_y_table():
    real, imag = y_columns()
    table = np.zeros((WY, WIN, 2, WY, HALF))
    for j in range(WY):
        table[j, :, 0, j] = real
        table[j, :, 1, j] = imag
    return split_table(table.reshape(2 * LANES, 2 * LANES))


def three_terms(table, axis):
    high, low = split_table(table)
    return np.concatenate([high, high, low], axis)


def z_inverse_table():
    angles = phase(np.outer(np.arange(SR) - SR // 2, Z_ORDER))
    four = np.eye(4)
    cosine, sine = np.kron(four, np.cos(angles)), np.kron(four, np.sin(angles))
    return three_terms(np.block([[cosine, -sine], [sine, cosine]]), 1)


def y_inverse_table():
    shifts = np.arange(SR) - SR // 2
    angles = phase(np.outer(np.arange(HALF), shifts))
    real, imag = 2.0 * np.cos(angles), -2.0 * np.sin(angles)
    real[0] = 1.0
    imag[0] = 1.0 - 2.0 * (shifts % 2)
    eight = np.eye(WY)
    table = np.concatenate([np.kron(eight, real), np.kron(eight, imag)], 0)
    return three_terms(table / WIN**3, 0)


def dot(a, b):
    return jnp.dot(a, b, preferred_element_type=F32)


def split(value, axis):
    high = value.astype(BF16)
    low = (value - high.astype(F32)).astype(BF16)
    return jnp.concatenate([high, low, high], axis)


def positions(shape):
    rows = lax.broadcasted_iota(jnp.int32, shape, len(shape) - 2)
    lanes = lax.broadcasted_iota(jnp.int32, shape, len(shape) - 1)
    return rows, lanes % HALF == 0


def z_stage(part_0, part_1, table_ref, real_ref, imag_ref, start):
    columns = [
        jnp.concatenate([part[:, :LANES], part[:, LANES:]], 0) for part in (part_0, part_1)
    ]
    slots = dot(table_ref[...], split(jnp.concatenate(columns, 1), 0))
    rows, zero_lane = positions((4, 8, LANES))
    mixed = [zero_lane & (rows != 0), zero_lane]
    weight = jnp.where(zero_lane & (rows == 0), 1.0, 2.0)
    no_mean = jnp.where(zero_lane & (rows == 0), 0.0, 2.0)
    energy = jnp.zeros((8, LANES), F32)
    for h in range(2):
        lanes = slice(h * LANES, (h + 1) * LANES)
        real = slots[: 4 * ZS, lanes].reshape(4, ZS, LANES)
        imag = slots[4 * ZS :, lanes].reshape(4, ZS, LANES)
        where_x = pl.ds(start + 4 * h, 4)
        for group in range(2):
            up = slice(group * 8, group * 8 + 8)
            down = slice(group * 8 + 16, group * 8 + 24)
            ur, ui, dr, di = real[:, up], imag[:, up], real[:, down], imag[:, down]
            mask = mixed[group]
            new = (
                jnp.where(mask, 0.5 * (ur + dr), ur),
                jnp.where(mask, 0.5 * (ui - di), ui),
                jnp.where(mask, 0.5 * (ui + di), dr),
                jnp.where(mask, 0.5 * (dr - ur), di),
            )
            real_ref[where_x, up] = new[0]
            imag_ref[where_x, up] = new[1]
            real_ref[where_x, down] = new[2]
            imag_ref[where_x, down] = new[3]
            if group == 0:
                parts = no_mean * new[0] * new[0] + weight * (
                    new[1] * new[1] + new[2] * new[2] + new[3] * new[3]
                )
            else:
                parts = 2.0 * sum(v * v for v in new)
            energy = energy + jnp.sum(parts, 0)
    return energy


def times(value, turn):
    real, imag = value
    eighth = round(8 * turn) % 8
    if abs(8 * turn - round(8 * turn)) > 1e-9:
        cosine, sine = math.cos(2.0 * math.pi * turn), math.sin(2.0 * math.pi * turn)
        return real * cosine - imag * sine, real * sine + imag * cosine
    if eighth % 2:
        half = math.sqrt(0.5)
        real, imag = half * (real - imag), half * (real + imag)
    quarter = eighth // 2
    if quarter == 1:
        return -imag, real
    if quarter == 2:
        return -real, -imag
    if quarter == 3:
        return imag, -real
    return real, imag


def plus(a, b):
    return a[0] + b[0], a[1] + b[1]


def minus(a, b):
    return a[0] - b[0], a[1] - b[1]


def fourier(values, sign):
    count = len(values)
    if count == 1:
        return values
    even, odd = fourier(values[0::2], sign), fourier(values[1::2], sign)
    odd = [times(value, sign * k / count) for k, value in enumerate(odd)]
    return [plus(a, b) for a, b in zip(even, odd)] + [minus(a, b) for a, b in zip(even, odd)]


def x_fourier(values):
    parts = [fourier([values(x + 8 * k) for k in range(4)], -1) for x in range(8)]
    parts = [[times(v, -x * b / WIN) for b, v in enumerate(part)] for x, part in enumerate(parts)]
    for b in range(4):
        yield fourier([parts[x][b] for x in range(8)], -1)


def special_lines(real_0, imag_0, real_16, imag_16):
    lane = lax.broadcasted_iota(jnp.int32, (WIN, LANES), 1) % HALF
    lines = jnp.where(lane == 0, real_0, 0.0)
    for n, line in enumerate((imag_0, real_16, imag_16)):
        lines = jnp.where(lane == n + 1, pltpu.roll(line, n + 1, 1), lines)
    means = jnp.sum(lines, 0, keepdims=True) * (1.0 / WIN)
    lines = jnp.where(lane == 0, lines - means, lines)
    return lines, jnp.sum(jnp.where(lane == 0, lines * lines, 0.0), 0, keepdims=True)


def variance(energy, mean_energy):
    total = jnp.sum(energy, 0, keepdims=True) + mean_energy
    total = jnp.broadcast_to(total, (8, LANES))
    group_row = lax.broadcasted_iota(jnp.int32, (LANES, LANES), 0) // HALF
    group_col = lax.broadcasted_iota(jnp.int32, (LANES, LANES), 1) // HALF
    same = (group_row == group_col).astype(F32)
    summed = jnp.dot(total, same, precision=lax.Precision.HIGHEST, preferred_element_type=F32)
    return summed * (1.0 / (ZS * WIN * WIN * ZS * WIN))


def first_tables(y_ref, z_ref):
    def halves(ref, rows, cols, value):
        high = value.astype(BF16)
        low = (value - high.astype(F32)).astype(BF16)
        for n, part in enumerate((high, low) if cols is None else (high, high, low)):
            if cols is None:
                ref[n * NY : (n + 1) * NY, rows] = part
            else:
                start = n * 2 * LANES
                ref[rows, start + cols.start : start + cols.stop] = part

    row = lax.broadcasted_iota(jnp.int32, (WIN, LANES), 0)
    lane = lax.broadcasted_iota(jnp.int32, (WIN, LANES), 1)
    unit = 2.0 * math.pi / WIN

    frequency = lane % HALF
    turns = (frequency * (row + STEP * (lane // HALF))) % WIN
    cosine = jnp.cos(turns.astype(F32) * unit)
    sine = jnp.where(frequency == 0, 2.0 * (row % 2).astype(F32) - 1.0, jnp.sin(turns.astype(F32) * unit))
    y = lax.broadcasted_iota(jnp.int32, (NY, LANES), 0)
    offset = y - STEP * (lax.broadcasted_iota(jnp.int32, (NY, LANES), 1) // HALF)
    inside = (offset >= 0) & (offset < WIN)
    for n, part in enumerate((cosine, -sine)):
        tall = jnp.concatenate([part] * (NY // WIN), 0)
        halves(y_ref, slice(n * LANES, (n + 1) * LANES), None, jnp.where(inside, tall, 0.0))

    order = jnp.where(row <= HALF, row, WIN + HALF - row)
    turns = (order * (lane % ZS)) % WIN
    cosine, sine = jnp.cos(turns.astype(F32) * unit), jnp.sin(turns.astype(F32) * unit)
    y_lane = lax.broadcasted_iota(jnp.int32, (4 * ZS, LANES), 1)
    same = lax.broadcasted_iota(jnp.int32, (4 * ZS, LANES), 0) // ZS == y_lane // ZS
    blocks = [jnp.where(same, jnp.concatenate([v] * 4, 0), 0.0) for v in (cosine, sine)]
    upper, lower = slice(0, LANES), slice(LANES, 2 * LANES)
    halves(z_ref, upper, upper, blocks[0])
    halves(z_ref, upper, lower, blocks[1])
    halves(z_ref, lower, upper, -blocks[1])
    halves(z_ref, lower, lower, blocks[0])


def first_stage(tile, y_ref, z_ref, real_ref, imag_ref, energy_ref):
    energy = jnp.zeros((8, LANES), F32)
    table = y_ref[...]
    for start in range(0, STEP, 8):
        rows = tile[start : start + 8].reshape(8 * ZS, NY)
        values = dot(jnp.concatenate([rows, rows], 1), table)
        energy = energy + z_stage(
            values[: 4 * ZS], values[4 * ZS :], z_ref, real_ref, imag_ref, start
        )
    energy_ref[...] = energy


def low_kernel(
    own_hbm,
    shift_x_hbm,
    shift_y_hbm,
    real_ref,
    imag_ref,
    energy_ref,
    y_ref,
    z_ref,
    shift_x_ref,
    shift_y_ref,
    own_ref,
    sems,
):
    copies = [
        pltpu.make_async_copy(own_hbm, own_ref, sems.at[0]),
        pltpu.make_async_copy(shift_x_hbm, shift_x_ref, sems.at[1]),
        pltpu.make_async_copy(shift_y_hbm, shift_y_ref, sems.at[2]),
    ]
    for copy in copies:
        copy.start()
    first_tables(y_ref, z_ref)
    for copy in copies:
        copy.wait()
    first_stage(own_ref[...], y_ref, z_ref, real_ref, imag_ref, energy_ref)


def high_kernel(
    next_ref,
    y_ref,
    z_ref,
    low_real_ref,
    low_imag_ref,
    low_energy_ref,
    real_ref,
    imag_ref,
    lines_ref,
    var_ref,
    high_real_ref,
    high_imag_ref,
    high_energy_ref,
):
    position = lax.axis_index("gx")
    inside = position < lax.axis_size("gx") - 1
    keep = jnp.where(inside, 1.0, 0.0).astype(BF16)
    tile = next_ref[...] * keep
    first_stage(tile, y_ref, z_ref, high_real_ref, high_imag_ref, high_energy_ref)

    def eight_slots(block, carry):
        where_z = pl.ds(pl.multiple_of(block * 8, 8), 8)

        def value(x):
            if x < STEP:
                return low_real_ref[x, where_z], low_imag_ref[x, where_z]
            return high_real_ref[x - STEP, where_z], high_imag_ref[x - STEP, where_z]

        for b, column in enumerate(x_fourier(value)):
            for a, (real, imag) in enumerate(column):
                real_ref[8 * b + a, where_z] = real
                imag_ref[8 * b + a, where_z] = imag
        return carry

    lax.fori_loop(0, ZS // 8, eight_slots, 0)
    lines = [
        jnp.concatenate([low[:, slot], high[:, slot]], 0)
        for slot in (0, HALF)
        for low, high in ((low_real_ref, high_real_ref), (low_imag_ref, high_imag_ref))
    ]
    lines_ref[...], mean_energy = special_lines(*lines)
    var_ref[...] = variance(low_energy_ref[...] + high_energy_ref[...], mean_energy)


def second_kernel(
    shift_x_ref,
    shift_y_ref,
    own_ref,
    mate_ref,
    near_own_ref,
    near_mate_ref,
    far_own_ref,
    far_mate_ref,
    mate_near_own_ref,
    mate_near_mate_ref,
    mate_far_own_ref,
    mate_far_mate_ref,
    first_real_ref,
    first_imag_ref,
    first_lines_ref,
    first_var_ref,
    y_high_ref,
    y_low_ref,
    z_ref,
    z_inverse_ref,
    y_inverse_ref,
    out_ref,
    region_ref,
    real_ref,
    imag_ref,
    cross_real_ref,
    cross_imag_ref,
    twice_ref,
):
    position = lax.axis_index("gx")
    tiles = lax.axis_size("gx")
    odd = position % 2
    even = 1 - odd
    tiles_below = position - odd - 4
    shifts_x, shifts_y = shift_x_ref[...], shift_y_ref[...]
    starts_x = [shifts_x[0, j] + STEP * (4 + odd) for j in range(WY)]
    starts_y = [shifts_y[0, j] + STEP * j for j in range(WY)]
    tiles_at = (
        (own_ref, 4 + odd),
        (mate_ref, 4 + even),
        (near_own_ref, 3 + 3 * even),
        (near_mate_ref, 2 + 5 * even),
        (far_own_ref, 1 + 7 * even),
        (far_mate_ref, 9 * even),
        (mate_near_own_ref, 3 + 3 * odd),
        (mate_near_mate_ref, 2 + 5 * odd),
        (mate_far_own_ref, 1 + 7 * odd),
        (mate_far_mate_ref, 9 * odd),
    )
    for tile_ref, at in tiles_at:
        region_ref[pl.ds(at * STEP, STEP)] = tile_ref[...]
    for tile in range(10):

        @pl.when((tiles_below + tile < 0) | (tiles_below + tile >= tiles))
        def _(tile=tile):
            region_ref[tile * STEP : (tile + 1) * STEP] = jnp.zeros((STEP, ZS, NY), BF16)

    lane = lax.broadcasted_iota(jnp.int32, (1, LANES), 1)

    def eight_x(step, energy):
        start = step * 8
        packs = []
        for half in range(2):
            total = None
            for n in range(4):
                j = half * 4 + n
                start_y = starts_y[j]
                block = region_ref[pl.ds(starts_x[j] + start, 8)].reshape(8 * ZS, NY)
                turned = pltpu.roll(block.astype(F32), (n * WIN - start_y) & (LANES - 1), 1)
                y = lane - n * WIN + start_y
                inside = (lane // WIN == n) & (y >= 0) & (y < NY)
                if total is None:
                    total = jnp.where(inside, turned, 0.0)
                else:
                    total = jnp.where(inside, turned, total)
            packs.append(total.astype(BF16))
        windows = jnp.concatenate(packs, 1)
        values = dot(windows, y_high_ref[...]) + dot(windows, y_low_ref[...])
        return energy + z_stage(
            values[: 4 * ZS], values[4 * ZS :], z_ref, real_ref, imag_ref, start
        )

    energy = lax.fori_loop(0, WIN // 8, eight_x, jnp.zeros((8, LANES), F32))
    def eight_slots(block, carry):
        where_z = pl.ds(pl.multiple_of(block * 8, 8), 8)

        def value(x):
            return real_ref[x, where_z], imag_ref[x, where_z]

        columns = []
        for b, column in enumerate(x_fourier(value)):
            cross = []
            for a, (gr, gi) in enumerate(column):
                fr, fi = first_real_ref[8 * b + a, where_z], first_imag_ref[8 * b + a, where_z]
                cross.append((fr * gr + fi * gi, fr * gi - fi * gr))
            column = fourier(cross, 1)
            columns.append([times(v, b * s / WIN) for s, v in enumerate(column)])
        for s in range(8):
            u = [column[s] for column in columns]
            even, odd = plus(u[0], u[2]), plus(u[1], u[3])
            here = plus(even, odd)
            even, odd = minus(u[0], u[2]), times(minus(u[1], u[3]), -0.25)
            back = plus(even, odd)
            cross_real_ref[8 + s, where_z], cross_imag_ref[8 + s, where_z] = here
            cross_real_ref[s, where_z], cross_imag_ref[s, where_z] = back
        return carry

    lax.fori_loop(0, ZS // 8, eight_slots, 0)

    lines, mean_energy = special_lines(
        real_ref[:, 0], imag_ref[:, 0], real_ref[:, HALF], imag_ref[:, HALF]
    )
    second_var = variance(energy, mean_energy)
    twice_ref[0:WIN] = lines
    twice_ref[WIN : 2 * WIN] = lines
    first_lines = first_lines_ref[...] * float(WIN)
    sums = []
    for s in range(SR):
        shift = (s - SR // 2) % WIN
        sums.append(
            jnp.sum(first_lines * twice_ref[shift : shift + WIN], 0, keepdims=True)
        )
    sums = jnp.concatenate(sums, 0)
    alone = [sums] + [pltpu.roll(sums, LANES - n, 1) for n in range(1, 4)]
    alone = [v.reshape(SR, 1, LANES) for v in alone]

    rows, zero_lane = positions((4, 8, LANES))
    special = zero_lane & (rows == 0)
    mixed = [zero_lane & (rows != 0), zero_lane]
    scale = 1.0 / (
        WIN**1.5 * (jnp.sqrt(first_var_ref[...] + 1e-6) * jnp.sqrt(second_var + 1e-6))
    )
    for start in range(0, SR, 8):
        columns = []
        for quarter in range(start, start + 8, 4):
            where_x = slice(quarter, quarter + 4)
            real = [None] * 4
            imag = [None] * 4
            for group in range(2):
                up = slice(group * 8, group * 8 + 8)
                down = slice(group * 8 + 16, group * 8 + 24)
                ur, ui = cross_real_ref[where_x, up], cross_imag_ref[where_x, up]
                dr, di = cross_real_ref[where_x, down], cross_imag_ref[where_x, down]
                mask = mixed[group]
                if group == 0:
                    ur, ui, dr, di = (
                        jnp.where(special, line[where_x], v)
                        for line, v in zip(alone, (ur, ui, dr, di))
                    )
                real[group] = jnp.where(mask, ur - di, ur)
                imag[group] = jnp.where(mask, ui + dr, ui)
                real[group + 2] = jnp.where(mask, ur + di, dr)
                imag[group + 2] = jnp.where(mask, dr - ui, di)
            columns.append(
                jnp.concatenate(
                    [jnp.concatenate(v, 1).reshape(4 * ZS, LANES) for v in (real, imag)], 0
                )
            )
        slots = dot(z_inverse_ref[...], split(jnp.concatenate(columns, 1), 0))
        for h in range(2):
            lanes = slice(h * LANES, (h + 1) * LANES)
            pair = jnp.concatenate([slots[: 4 * SR, lanes], slots[4 * SR :, lanes]], 1)
            values = dot(split(pair, 1), y_inverse_ref[...])
            where_out = slice((start + 4 * h) * SR, (start + 4 * h + 4) * SR)
            out_ref[where_out] = values * scale[0:1]


def product_kernel(own_ref, mate_ref, other_ref, out_ref):
    position = lax.axis_index("gx")
    edge = (position == 0) | (position == lax.axis_size("gx") - 1)
    own = own_ref[...]
    lane = lax.broadcasted_iota(jnp.int32, own.shape, 1)
    below = jnp.where(lane < SR, 1.0, pltpu.roll(own, SR, 1))
    above = jnp.where(lane >= LANES - SR, 1.0, pltpu.roll(own, LANES - SR, 1))
    other = jnp.where(edge, 1.0, other_ref[...])
    out_ref[...] = own * mate_ref[...] * other * below * above


def params():
    return pltpu.CompilerParams(vmem_limit_bytes=VMEM_LIMIT)


VMEM = pl.BlockSpec(memory_space=pltpu.VMEM)
HBM = pl.BlockSpec(memory_space=pltpu.HBM)


def local(first_volume, second_volume, shift_x, shift_y):
    size = lax.axis_size("gx")
    chips = size // 2

    def send(value, pairs):
        return lax.ppermute(value, "gx", pairs)

    last = size - 1
    mates = [(i, i ^ 1) for i in range(size)]
    near = [(2 * q + 2, 2 * q) for q in range(chips - 1)] + [(last, last - 1)]
    near += [(2 * q - 1, 2 * q + 1) for q in range(1, chips)] + [(0, 1)]
    far = [(2 * q + 4, 2 * q) for q in range(chips - 2)] + [(last, last - 1), (last - 2, last - 3)]
    far += [(2 * q - 3, 2 * q + 1) for q in range(2, chips)] + [(0, 1), (2, 3)]
    across = [(i, i + 1 if i % 2 else i - 1) for i in range(1, last)] + [(0, 0), (last, last)]

    next_tile = send(first_volume, [((i + 1) % size, i) for i in range(size)])
    near_own = send(second_volume, near)
    mate_tile = send(second_volume, mates)
    far_own = send(second_volume, far)
    mate_first = send(first_volume, mates)
    low_tile = first_volume
    low_tile, mate_tile = lax.optimization_barrier((first_volume, mate_tile))
    near_mate = send(mate_tile, near)
    far_mate = send(mate_tile, far)

    half = jax.ShapeDtypeStruct((STEP, ZS, LANES), F32)
    whole = jax.ShapeDtypeStruct((WIN, ZS, LANES), F32)
    lines = jax.ShapeDtypeStruct((WIN, LANES), F32)
    row = jax.ShapeDtypeStruct((8, LANES), F32)
    y_table = jax.ShapeDtypeStruct((2 * NY, 2 * LANES), BF16)
    z_table = jax.ShapeDtypeStruct((2 * LANES, 6 * LANES), BF16)
    shifts = [jax.ShapeDtypeStruct(v.shape, v.dtype) for v in (shift_x, shift_y)]

    def first_spectra(kernel, specs, outs, scratch, *operands):
        return pl.pallas_call(
            kernel,
            out_shape=outs,
            in_specs=specs,
            out_specs=(VMEM,) * len(outs),
            scratch_shapes=scratch,
            compiler_params=params(),
            cost_estimate=pl.CostEstimate(
                flops=2 * 10**9, transcendentals=0, bytes_accessed=2 * 10**6
            ),
            name="first_spectra",
        )(*operands)

    *low_part, y_table, z_table, shift_x, shift_y = first_spectra(
        low_kernel,
        [HBM] * 3,
        (half, half, row, y_table, z_table, *shifts),
        [pltpu.VMEM(first_volume.shape, BF16), pltpu.SemaphoreType.DMA((3,))],
        *(
            pltpu.with_memory_space_constraint(v, pltpu.HBM)
            for v in (first_volume, shift_x, shift_y)
        ),
    )
    near_own, *low_part = lax.optimization_barrier((near_own, *low_part))
    first_part = first_spectra(
        high_kernel,
        [VMEM] * 6,
        (whole, whole, lines, row),
        [pltpu.VMEM(v.shape, F32) for v in (half, half, row)],
        next_tile,
        y_table,
        z_table,
        *low_part,
    )
    side = (near_own, near_mate, far_own, far_mate)
    mate_side = [send(tile, mates) for tile in side]

    y_high, y_low = second_y_table()
    maps = pl.pallas_call(
        second_kernel,
        out_shape=jax.ShapeDtypeStruct((SR * SR, LANES), F32),
        in_specs=[VMEM] * 21,
        out_specs=VMEM,
        scratch_shapes=[
            pltpu.VMEM((10 * STEP, ZS, NY), BF16),
            pltpu.VMEM((WIN, ZS, LANES), F32),
            pltpu.VMEM((WIN, ZS, LANES), F32),
            pltpu.VMEM((SR, ZS, LANES), F32),
            pltpu.VMEM((SR, ZS, LANES), F32),
            pltpu.VMEM((2 * WIN, LANES), F32),
        ],
        compiler_params=params(),
        name="second_maps",
    )(
        shift_x,
        shift_y,
        second_volume,
        mate_tile,
        *side,
        *mate_side,
        *first_part,
        y_high,
        y_low,
        z_table,
        z_inverse_table(),
        y_inverse_table(),
    )

    other_maps = send(maps, across)
    mate_maps = send(maps, mates)
    product = pl.pallas_call(
        product_kernel,
        out_shape=jax.ShapeDtypeStruct((SR * SR, LANES), F32),
        in_specs=[VMEM] * 3,
        out_specs=VMEM,
        compiler_params=params(),
        name="product",
    )(maps, mate_maps, other_maps)
    return product.reshape(1, SR, SR, LANES)


def solution(mesh):
    return jax.shard_map(
        local,
        mesh=mesh,
        in_specs=(
            P(("groups", "gx"), None, None),
            P(("groups", "gx"), None, None),
            P(("groups", "gx"), None),
            P(("groups", "gx"), None),
        ),
        out_specs=P(("groups", "gx"), None, None, None),
        check_vma=False,
    )
```

```python
import math

import jax
import jax.numpy as jnp
import numpy as np
from jax import lax
from jax.experimental import pallas as pl
from jax.experimental.pallas import tpu as pltpu
from jax.sharding import PartitionSpec as P

WIN = 32
STEP = 16
ZS = 32
SR = 16
WY = 8
NY = WY * STEP
LANES = 128
HALF = WIN // 2
BF16 = jnp.bfloat16
F32 = jnp.float32
VMEM_LIMIT = 48 * 2**20

Z_ORDER = np.array([*range(16), 16, *range(31, 16, -1)])


def split_table(table):
    high = np.asarray(table, np.float32).astype(BF16)
    low = (np.asarray(table, np.float64) - high.astype(np.float64)).astype(BF16)
    return high, low


def phase(numbers):
    return 2.0 * math.pi * (np.asarray(numbers) % WIN) / WIN


def y_columns():
    angles = phase(np.outer(np.arange(WIN), np.arange(HALF)))
    real, imag = np.cos(angles), -np.sin(angles)
    imag[:, 0] = 1.0 - 2.0 * (np.arange(WIN) % 2)
    return real, imag


def second_y_table():
    real, imag = y_columns()
    table = np.zeros((WY, WIN, 2, WY, HALF))
    for j in range(WY):
        table[j, :, 0, j] = real
        table[j, :, 1, j] = imag
    return split_table(table.reshape(2 * LANES, 2 * LANES))


def three_terms(table, axis):
    high, low = split_table(table)
    return np.concatenate([high, high, low], axis)


def z_inverse_table():
    angles = phase(np.outer(np.arange(SR) - SR // 2, Z_ORDER))
    four = np.eye(4)
    cosine, sine = np.kron(four, np.cos(angles)), np.kron(four, np.sin(angles))
    return three_terms(np.block([[cosine, -sine], [sine, cosine]]), 1)


def y_inverse_table():
    shifts = np.arange(SR) - SR // 2
    angles = phase(np.outer(np.arange(HALF), shifts))
    real, imag = 2.0 * np.cos(angles), -2.0 * np.sin(angles)
    real[0] = 1.0
    imag[0] = 1.0 - 2.0 * (shifts % 2)
    eight = np.eye(WY)
    table = np.concatenate([np.kron(eight, real), np.kron(eight, imag)], 0)
    return three_terms(table / WIN**3, 0)


def dot(a, b):
    return jnp.dot(a, b, preferred_element_type=F32)


def split(value, axis):
    high = value.astype(BF16)
    low = (value - high.astype(F32)).astype(BF16)
    return jnp.concatenate([high, low, high], axis)


def positions(shape):
    rows = lax.broadcasted_iota(jnp.int32, shape, len(shape) - 2)
    lanes = lax.broadcasted_iota(jnp.int32, shape, len(shape) - 1)
    return rows, lanes % HALF == 0


def z_stage(part_0, part_1, table_ref, real_ref, imag_ref, start):
    columns = [
        jnp.concatenate([part[:, :LANES], part[:, LANES:]], 0) for part in (part_0, part_1)
    ]
    slots = dot(table_ref[...], split(jnp.concatenate(columns, 1), 0))
    rows, zero_lane = positions((4, 8, LANES))
    mixed = [zero_lane & (rows != 0), zero_lane]
    weight = jnp.where(zero_lane & (rows == 0), 1.0, 2.0)
    no_mean = jnp.where(zero_lane & (rows == 0), 0.0, 2.0)
    energy = jnp.zeros((8, LANES), F32)
    for h in range(2):
        lanes = slice(h * LANES, (h + 1) * LANES)
        real = slots[: 4 * ZS, lanes].reshape(4, ZS, LANES)
        imag = slots[4 * ZS :, lanes].reshape(4, ZS, LANES)
        where_x = pl.ds(start + 4 * h, 4)
        for group in range(2):
            up = slice(group * 8, group * 8 + 8)
            down = slice(group * 8 + 16, group * 8 + 24)
            ur, ui, dr, di = real[:, up], imag[:, up], real[:, down], imag[:, down]
            mask = mixed[group]
            new = (
                jnp.where(mask, 0.5 * (ur + dr), ur),
                jnp.where(mask, 0.5 * (ui - di), ui),
                jnp.where(mask, 0.5 * (ui + di), dr),
                jnp.where(mask, 0.5 * (dr - ur), di),
            )
            real_ref[where_x, up] = new[0]
            imag_ref[where_x, up] = new[1]
            real_ref[where_x, down] = new[2]
            imag_ref[where_x, down] = new[3]
            if group == 0:
                parts = no_mean * new[0] * new[0] + weight * (
                    new[1] * new[1] + new[2] * new[2] + new[3] * new[3]
                )
            else:
                parts = 2.0 * sum(v * v for v in new)
            energy = energy + jnp.sum(parts, 0)
    return energy


def times(value, turn):
    real, imag = value
    eighth = round(8 * turn) % 8
    if abs(8 * turn - round(8 * turn)) > 1e-9:
        cosine, sine = math.cos(2.0 * math.pi * turn), math.sin(2.0 * math.pi * turn)
        return real * cosine - imag * sine, real * sine + imag * cosine
    if eighth % 2:
        half = math.sqrt(0.5)
        real, imag = half * (real - imag), half * (real + imag)
    quarter = eighth // 2
    if quarter == 1:
        return -imag, real
    if quarter == 2:
        return -real, -imag
    if quarter == 3:
        return imag, -real
    return real, imag


def plus(a, b):
    return a[0] + b[0], a[1] + b[1]


def minus(a, b):
    return a[0] - b[0], a[1] - b[1]


def fourier(values, sign):
    count = len(values)
    if count == 1:
        return values
    even, odd = fourier(values[0::2], sign), fourier(values[1::2], sign)
    odd = [times(value, sign * k / count) for k, value in enumerate(odd)]
    return [plus(a, b) for a, b in zip(even, odd)] + [minus(a, b) for a, b in zip(even, odd)]


def x_fourier(values):
    parts = [fourier([values(x + 8 * k) for k in range(4)], -1) for x in range(8)]
    parts = [[times(v, -x * b / WIN) for b, v in enumerate(part)] for x, part in enumerate(parts)]
    for b in range(4):
        yield fourier([parts[x][b] for x in range(8)], -1)


def special_lines(real_0, imag_0, real_16, imag_16):
    lane = lax.broadcasted_iota(jnp.int32, (WIN, LANES), 1) % HALF
    lines = jnp.where(lane == 0, real_0, 0.0)
    for n, line in enumerate((imag_0, real_16, imag_16)):
        lines = jnp.where(lane == n + 1, pltpu.roll(line, n + 1, 1), lines)
    means = jnp.sum(lines, 0, keepdims=True) * (1.0 / WIN)
    lines = jnp.where(lane == 0, lines - means, lines)
    return lines, jnp.sum(jnp.where(lane == 0, lines * lines, 0.0), 0, keepdims=True)


def variance(energy, mean_energy):
    total = jnp.sum(energy, 0, keepdims=True) + mean_energy
    total = jnp.broadcast_to(total, (8, LANES))
    group_row = lax.broadcasted_iota(jnp.int32, (LANES, LANES), 0) // HALF
    group_col = lax.broadcasted_iota(jnp.int32, (LANES, LANES), 1) // HALF
    same = (group_row == group_col).astype(F32)
    summed = jnp.dot(total, same, precision=lax.Precision.HIGHEST, preferred_element_type=F32)
    return summed * (1.0 / (ZS * WIN * WIN * ZS * WIN))


def first_tables(y_ref, z_ref):
    def halves(ref, rows, cols, value):
        high = value.astype(BF16)
        low = (value - high.astype(F32)).astype(BF16)
        for n, part in enumerate((high, low) if cols is None else (high, high, low)):
            if cols is None:
                ref[n * NY : (n + 1) * NY, rows] = part
            else:
                start = n * 2 * LANES
                ref[rows, start + cols.start : start + cols.stop] = part

    row = lax.broadcasted_iota(jnp.int32, (WIN, LANES), 0)
    lane = lax.broadcasted_iota(jnp.int32, (WIN, LANES), 1)
    unit = 2.0 * math.pi / WIN

    frequency = lane % HALF
    turns = (frequency * (row + STEP * (lane // HALF))) % WIN
    cosine = jnp.cos(turns.astype(F32) * unit)
    sine = jnp.where(frequency == 0, 2.0 * (row % 2).astype(F32) - 1.0, jnp.sin(turns.astype(F32) * unit))
    y = lax.broadcasted_iota(jnp.int32, (NY, LANES), 0)
    offset = y - STEP * (lax.broadcasted_iota(jnp.int32, (NY, LANES), 1) // HALF)
    inside = (offset >= 0) & (offset < WIN)
    for n, part in enumerate((cosine, -sine)):
        tall = jnp.concatenate([part] * (NY // WIN), 0)
        halves(y_ref, slice(n * LANES, (n + 1) * LANES), None, jnp.where(inside, tall, 0.0))

    order = jnp.where(row <= HALF, row, WIN + HALF - row)
    turns = (order * (lane % ZS)) % WIN
    cosine, sine = jnp.cos(turns.astype(F32) * unit), jnp.sin(turns.astype(F32) * unit)
    y_lane = lax.broadcasted_iota(jnp.int32, (4 * ZS, LANES), 1)
    same = lax.broadcasted_iota(jnp.int32, (4 * ZS, LANES), 0) // ZS == y_lane // ZS
    blocks = [jnp.where(same, jnp.concatenate([v] * 4, 0), 0.0) for v in (cosine, sine)]
    upper, lower = slice(0, LANES), slice(LANES, 2 * LANES)
    halves(z_ref, upper, upper, blocks[0])
    halves(z_ref, upper, lower, blocks[1])
    halves(z_ref, lower, upper, -blocks[1])
    halves(z_ref, lower, lower, blocks[0])


def first_stage(tile, y_ref, z_ref, real_ref, imag_ref, energy_ref):
    energy = jnp.zeros((8, LANES), F32)
    table = y_ref[...]
    for start in range(0, STEP, 8):
        rows = tile[start : start + 8].reshape(8 * ZS, NY)
        values = dot(jnp.concatenate([rows, rows], 1), table)
        energy = energy + z_stage(
            values[: 4 * ZS], values[4 * ZS :], z_ref, real_ref, imag_ref, start
        )
    energy_ref[...] = energy


def low_kernel(
    tile_ref,
    shift_x_hbm,
    shift_y_hbm,
    real_ref,
    imag_ref,
    energy_ref,
    y_ref,
    z_ref,
    shifts_ref,
    shift_x_ref,
    shift_y_ref,
    sems,
):
    copies = [
        pltpu.make_async_copy(shift_x_hbm, shift_x_ref, sems.at[0]),
        pltpu.make_async_copy(shift_y_hbm, shift_y_ref, sems.at[1]),
    ]
    for copy in copies:
        copy.start()
    first_tables(y_ref, z_ref)
    first_stage(tile_ref[...], y_ref, z_ref, real_ref, imag_ref, energy_ref)
    for copy in copies:
        copy.wait()
    shifts_ref[0:1] = shift_x_ref[...]
    shifts_ref[1:2] = shift_y_ref[...]


def high_kernel(
    next_ref,
    own_ref,
    y_ref,
    z_ref,
    low_real_ref,
    low_imag_ref,
    low_energy_ref,
    real_ref,
    imag_ref,
    lines_ref,
    var_ref,
    high_real_ref,
    high_imag_ref,
    high_energy_ref,
):
    position = lax.axis_index("gx")
    odd = position % 2
    inside = position < lax.axis_size("gx") - 2
    use_next = jnp.where(inside & (odd == 0), 1.0, 0.0).astype(BF16)
    use_own = odd.astype(BF16)
    tile = next_ref[...] * use_next + own_ref[...] * use_own
    first_stage(tile, y_ref, z_ref, high_real_ref, high_imag_ref, high_energy_ref)

    def eight_slots(where_z):
        def value(x):
            if x < STEP:
                return low_real_ref[x, where_z], low_imag_ref[x, where_z]
            return high_real_ref[x - STEP, where_z], high_imag_ref[x - STEP, where_z]

        for b, column in enumerate(x_fourier(value)):
            for a, (real, imag) in enumerate(column):
                real_ref[8 * b + a, where_z] = real
                imag_ref[8 * b + a, where_z] = imag

    for start in range(0, ZS, 8):
        eight_slots(slice(start, start + 8))
    lines = [
        jnp.concatenate([low[:, slot], high[:, slot]], 0)
        for slot in (0, HALF)
        for low, high in ((low_real_ref, high_real_ref), (low_imag_ref, high_imag_ref))
    ]
    lines_ref[...], mean_energy = special_lines(*lines)
    var_ref[...] = variance(low_energy_ref[...] + high_energy_ref[...], mean_energy)


def second_kernel(
    shifts_ref,
    own_ref,
    mate_ref,
    near_own_ref,
    near_mate_ref,
    far_own_ref,
    far_mate_ref,
    mate_near_own_ref,
    mate_near_mate_ref,
    mate_far_own_ref,
    mate_far_mate_ref,
    first_real_ref,
    first_imag_ref,
    first_lines_ref,
    first_var_ref,
    y_high_ref,
    y_low_ref,
    z_ref,
    z_inverse_ref,
    y_inverse_ref,
    out_ref,
    region_ref,
    real_ref,
    imag_ref,
    cross_real_ref,
    cross_imag_ref,
    twice_ref,
):
    position = lax.axis_index("gx")
    tiles = lax.axis_size("gx")
    odd = position % 2
    even = 1 - odd
    tiles_below = position - odd - 4
    shifts = shifts_ref[...]
    starts_x = [shifts[0, j] + STEP * (4 + even) for j in range(WY)]
    starts_y = [shifts[1, j] + STEP * j for j in range(WY)]
    tiles_at = (
        (own_ref, 4 + odd),
        (mate_ref, 4 + even),
        (near_own_ref, 3 + 3 * even),
        (near_mate_ref, 2 + 5 * even),
        (far_own_ref, 1 + 7 * even),
        (far_mate_ref, 9 * even),
        (mate_near_own_ref, 3 + 3 * odd),
        (mate_near_mate_ref, 2 + 5 * odd),
        (mate_far_own_ref, 1 + 7 * odd),
        (mate_far_mate_ref, 9 * odd),
    )
    for tile_ref, at in tiles_at:
        region_ref[pl.ds(at * STEP, STEP)] = tile_ref[...]
    for tile in range(10):

        @pl.when((tiles_below + tile < 0) | (tiles_below + tile >= tiles))
        def _(tile=tile):
            region_ref[tile * STEP : (tile + 1) * STEP] = jnp.zeros((STEP, ZS, NY), BF16)

    lane = lax.broadcasted_iota(jnp.int32, (1, LANES), 1)

    def eight_x(start, energy):
        packs = []
        for half in range(2):
            total = None
            for n in range(4):
                j = half * 4 + n
                start_y = starts_y[j]
                block = region_ref[pl.ds(starts_x[j] + start, 8)].reshape(8 * ZS, NY)
                turned = pltpu.roll(block.astype(F32), (n * WIN - start_y) & (LANES - 1), 1)
                y = lane - n * WIN + start_y
                inside = (lane // WIN == n) & (y >= 0) & (y < NY)
                if total is None:
                    total = jnp.where(inside, turned, 0.0)
                else:
                    total = jnp.where(inside, turned, total)
            packs.append(total.astype(BF16))
        windows = jnp.concatenate(packs, 1)
        values = dot(windows, y_high_ref[...]) + dot(windows, y_low_ref[...])
        return energy + z_stage(
            values[: 4 * ZS], values[4 * ZS :], z_ref, real_ref, imag_ref, start
        )

    energy = jnp.zeros((8, LANES), F32)
    for start in range(0, WIN, 8):
        energy = eight_x(start, energy)
    def eight_slots(where_z):
        def value(x):
            return real_ref[x, where_z], imag_ref[x, where_z]

        columns = []
        for b, column in enumerate(x_fourier(value)):
            cross = []
            for a, (gr, gi) in enumerate(column):
                fr, fi = first_real_ref[8 * b + a, where_z], first_imag_ref[8 * b + a, where_z]
                cross.append((fr * gr + fi * gi, fr * gi - fi * gr))
            column = fourier(cross, 1)
            columns.append([times(v, b * s / WIN) for s, v in enumerate(column)])
        for s in range(8):
            u = [column[s] for column in columns]
            even, odd = plus(u[0], u[2]), plus(u[1], u[3])
            here = plus(even, odd)
            even, odd = minus(u[0], u[2]), times(minus(u[1], u[3]), -0.25)
            back = plus(even, odd)
            cross_real_ref[8 + s, where_z], cross_imag_ref[8 + s, where_z] = here
            cross_real_ref[s, where_z], cross_imag_ref[s, where_z] = back

    for start in range(0, ZS, 8):
        eight_slots(slice(start, start + 8))

    lines, mean_energy = special_lines(
        real_ref[:, 0], imag_ref[:, 0], real_ref[:, HALF], imag_ref[:, HALF]
    )
    second_var = variance(energy, mean_energy)
    twice_ref[0:WIN] = lines
    twice_ref[WIN : 2 * WIN] = lines
    first_lines = first_lines_ref[...] * float(WIN)
    sums = []
    for s in range(SR):
        shift = (s - SR // 2) % WIN
        sums.append(
            jnp.sum(first_lines * twice_ref[shift : shift + WIN], 0, keepdims=True)
        )
    sums = jnp.concatenate(sums, 0)
    alone = [sums] + [pltpu.roll(sums, LANES - n, 1) for n in range(1, 4)]
    alone = [v.reshape(SR, 1, LANES) for v in alone]

    rows, zero_lane = positions((4, 8, LANES))
    special = zero_lane & (rows == 0)
    mixed = [zero_lane & (rows != 0), zero_lane]
    scale = 1.0 / (
        WIN**1.5 * (jnp.sqrt(first_var_ref[...] + 1e-6) * jnp.sqrt(second_var + 1e-6))
    )
    for start in range(0, SR, 8):
        columns = []
        for quarter in range(start, start + 8, 4):
            where_x = slice(quarter, quarter + 4)
            real = [None] * 4
            imag = [None] * 4
            for group in range(2):
                up = slice(group * 8, group * 8 + 8)
                down = slice(group * 8 + 16, group * 8 + 24)
                ur, ui = cross_real_ref[where_x, up], cross_imag_ref[where_x, up]
                dr, di = cross_real_ref[where_x, down], cross_imag_ref[where_x, down]
                mask = mixed[group]
                if group == 0:
                    ur, ui, dr, di = (
                        jnp.where(special, line[where_x], v)
                        for line, v in zip(alone, (ur, ui, dr, di))
                    )
                real[group] = jnp.where(mask, ur - di, ur)
                imag[group] = jnp.where(mask, ui + dr, ui)
                real[group + 2] = jnp.where(mask, ur + di, dr)
                imag[group + 2] = jnp.where(mask, dr - ui, di)
            columns.append(
                jnp.concatenate(
                    [jnp.concatenate(v, 1).reshape(4 * ZS, LANES) for v in (real, imag)], 0
                )
            )
        slots = dot(z_inverse_ref[...], split(jnp.concatenate(columns, 1), 0))
        for h in range(2):
            lanes = slice(h * LANES, (h + 1) * LANES)
            pair = jnp.concatenate([slots[: 4 * SR, lanes], slots[4 * SR :, lanes]], 1)
            values = dot(split(pair, 1), y_inverse_ref[...])
            where_out = slice((start + 4 * h) * SR, (start + 4 * h + 4) * SR)
            out_ref[where_out] = values * scale[0:1]


def product_kernel(made_ref, own_ref, other_ref, out_ref):
    position = lax.axis_index("gx")
    edge = (position == 0) | (position == lax.axis_size("gx") - 1)
    own = own_ref[...]
    lane = lax.broadcasted_iota(jnp.int32, own.shape, 1)
    below = jnp.where(lane < SR, 1.0, pltpu.roll(own, SR, 1))
    above = jnp.where(lane >= LANES - SR, 1.0, pltpu.roll(own, LANES - SR, 1))
    other = jnp.where(edge, 1.0, other_ref[...])
    out_ref[...] = own * made_ref[...] * other * below * above


def params():
    return pltpu.CompilerParams(vmem_limit_bytes=VMEM_LIMIT)


VMEM = pl.BlockSpec(memory_space=pltpu.VMEM)
HBM = pl.BlockSpec(memory_space=pltpu.HBM)


def local(first_volume, second_volume, shift_x, shift_y):
    size = lax.axis_size("gx")
    chips = size // 2

    def send(value, pairs):
        return lax.ppermute(value, "gx", pairs)

    last = size - 1
    mates = [(i, i ^ 1) for i in range(size)]
    near = [(2 * q + 2, 2 * q) for q in range(chips - 1)] + [(last, last - 1)]
    near += [(2 * q - 1, 2 * q + 1) for q in range(1, chips)] + [(0, 1)]
    far = [(2 * q + 4, 2 * q) for q in range(chips - 2)] + [(last, last - 1), (last - 2, last - 3)]
    far += [(2 * q - 3, 2 * q + 1) for q in range(2, chips)] + [(0, 1), (2, 3)]
    near_own = send(second_volume, near)
    mate_tile = send(second_volume, mates)
    far_own = send(second_volume, far)
    near_first = send(first_volume, near)
    mate_first = send(first_volume, mates)
    near_mate = send(mate_tile, near)
    far_mate = send(mate_tile, far)

    half = jax.ShapeDtypeStruct((STEP, ZS, LANES), F32)
    whole = jax.ShapeDtypeStruct((WIN, ZS, LANES), F32)
    lines = jax.ShapeDtypeStruct((WIN, LANES), F32)
    row = jax.ShapeDtypeStruct((8, LANES), F32)
    y_table = jax.ShapeDtypeStruct((2 * NY, 2 * LANES), BF16)
    z_table = jax.ShapeDtypeStruct((2 * LANES, 6 * LANES), BF16)
    shifts = jax.ShapeDtypeStruct((2, WY), shift_x.dtype)

    def first_spectra(kernel, specs, outs, scratch, *operands):
        return pl.pallas_call(
            kernel,
            out_shape=outs,
            in_specs=specs,
            out_specs=(VMEM,) * len(outs),
            scratch_shapes=scratch,
            compiler_params=params(),
            cost_estimate=pl.CostEstimate(
                flops=2 * 10**9, transcendentals=0, bytes_accessed=2 * 10**6
            ),
            name="first_spectra",
        )(*operands)

    *low_part, y_table, z_table, shifts = first_spectra(
        low_kernel,
        [VMEM] + [HBM] * 2,
        (half, half, row, y_table, z_table, shifts),
        [pltpu.VMEM(v.shape, v.dtype) for v in (shift_x, shift_y)]
        + [pltpu.SemaphoreType.DMA((2,))],
        mate_first,
        *(pltpu.with_memory_space_constraint(v, pltpu.HBM) for v in (shift_x, shift_y)),
    )
    near_own, *low_part = lax.optimization_barrier((near_own, *low_part))
    first_part = first_spectra(
        high_kernel,
        [VMEM] * 7,
        (whole, whole, lines, row),
        [pltpu.VMEM(v.shape, F32) for v in (half, half, row)],
        near_first,
        first_volume,
        y_table,
        z_table,
        *low_part,
    )
    side = (near_own, near_mate, far_own, far_mate)
    mate_side = [send(tile, mates) for tile in side]

    y_high, y_low = second_y_table()
    maps = pl.pallas_call(
        second_kernel,
        out_shape=jax.ShapeDtypeStruct((SR * SR, LANES), F32),
        in_specs=[VMEM] * 20,
        out_specs=VMEM,
        scratch_shapes=[
            pltpu.VMEM((10 * STEP, ZS, NY), BF16),
            pltpu.VMEM((WIN, ZS, LANES), F32),
            pltpu.VMEM((WIN, ZS, LANES), F32),
            pltpu.VMEM((SR, ZS, LANES), F32),
            pltpu.VMEM((SR, ZS, LANES), F32),
            pltpu.VMEM((2 * WIN, LANES), F32),
        ],
        compiler_params=params(),
        name="second_maps",
    )(
        send(shifts, mates),
        second_volume,
        mate_tile,
        *side,
        *mate_side,
        *first_part,
        y_high,
        y_low,
        z_table,
        z_inverse_table(),
        y_inverse_table(),
    )

    own_maps = send(maps, mates)
    other_maps = send(maps, [(b, a) for a, b in near])
    product = pl.pallas_call(
        product_kernel,
        out_shape=jax.ShapeDtypeStruct((SR * SR, LANES), F32),
        in_specs=[VMEM] * 3,
        out_specs=VMEM,
        compiler_params=params(),
        name="product",
    )(maps, own_maps, other_maps)
    return product.reshape(1, SR, SR, LANES)


def solution(mesh):
    return jax.shard_map(
        local,
        mesh=mesh,
        in_specs=(
            P(("groups", "gx"), None, None),
            P(("groups", "gx"), None, None),
            P(("groups", "gx"), None),
            P(("groups", "gx"), None),
        ),
        out_specs=P(("groups", "gx"), None, None, None),
        check_vma=False,
    )
```

```python
import math

import jax
import jax.numpy as jnp
import numpy as np
from jax import lax
from jax.experimental import pallas as pl
from jax.experimental.pallas import tpu as pltpu
from jax.sharding import PartitionSpec as P

WIN = 32
STEP = 16
ZS = 32
SR = 16
WY = 8
NY = WY * STEP
LANES = 128
HALF = WIN // 2
BF16 = jnp.bfloat16
F32 = jnp.float32
VMEM_LIMIT = 48 * 2**20

Z_ORDER = np.array([*range(16), 16, *range(31, 16, -1)])


def split_table(table):
    high = np.asarray(table, np.float32).astype(BF16)
    low = (np.asarray(table, np.float64) - high.astype(np.float64)).astype(BF16)
    return high, low


def phase(numbers):
    return 2.0 * math.pi * (np.asarray(numbers) % WIN) / WIN


def y_columns():
    angles = phase(np.outer(np.arange(WIN), np.arange(HALF)))
    real, imag = np.cos(angles), -np.sin(angles)
    imag[:, 0] = 1.0 - 2.0 * (np.arange(WIN) % 2)
    return real, imag


def second_y_table():
    real, imag = y_columns()
    table = np.zeros((WY, WIN, 2, WY, HALF))
    for j in range(WY):
        table[j, :, 0, j] = real
        table[j, :, 1, j] = imag
    return split_table(table.reshape(2 * LANES, 2 * LANES))


def three_terms(table, axis):
    high, low = split_table(table)
    return np.concatenate([high, high, low], axis)


def z_inverse_table():
    angles = phase(np.outer(np.arange(SR) - SR // 2, Z_ORDER))
    four = np.eye(4)
    cosine, sine = np.kron(four, np.cos(angles)), np.kron(four, np.sin(angles))
    return three_terms(np.block([[cosine, -sine], [sine, cosine]]), 1)


def y_inverse_table():
    shifts = np.arange(SR) - SR // 2
    angles = phase(np.outer(np.arange(HALF), shifts))
    real, imag = 2.0 * np.cos(angles), -2.0 * np.sin(angles)
    real[0] = 1.0
    imag[0] = 1.0 - 2.0 * (shifts % 2)
    eight = np.eye(WY)
    table = np.concatenate([np.kron(eight, real), np.kron(eight, imag)], 0)
    return three_terms(table / WIN**3, 0)


def dot(a, b):
    return jnp.dot(a, b, preferred_element_type=F32)


def split(value, axis):
    high = value.astype(BF16)
    low = (value - high.astype(F32)).astype(BF16)
    return jnp.concatenate([high, low, high], axis)


def positions(shape):
    rows = lax.broadcasted_iota(jnp.int32, shape, len(shape) - 2)
    lanes = lax.broadcasted_iota(jnp.int32, shape, len(shape) - 1)
    return rows, lanes % HALF == 0


def z_stage(part_0, part_1, table_ref, real_ref, imag_ref, start):
    columns = [
        jnp.concatenate([part[:, :LANES], part[:, LANES:]], 0) for part in (part_0, part_1)
    ]
    slots = dot(table_ref[...], split(jnp.concatenate(columns, 1), 0))
    rows, zero_lane = positions((4, 8, LANES))
    mixed = [zero_lane & (rows != 0), zero_lane]
    weight = jnp.where(zero_lane & (rows == 0), 1.0, 2.0)
    no_mean = jnp.where(zero_lane & (rows == 0), 0.0, 2.0)
    energy = jnp.zeros((8, LANES), F32)
    for h in range(2):
        lanes = slice(h * LANES, (h + 1) * LANES)
        real = slots[: 4 * ZS, lanes].reshape(4, ZS, LANES)
        imag = slots[4 * ZS :, lanes].reshape(4, ZS, LANES)
        where_x = pl.ds(start + 4 * h, 4)
        for group in range(2):
            up = slice(group * 8, group * 8 + 8)
            down = slice(group * 8 + 16, group * 8 + 24)
            ur, ui, dr, di = real[:, up], imag[:, up], real[:, down], imag[:, down]
            mask = mixed[group]
            new = (
                jnp.where(mask, 0.5 * (ur + dr), ur),
                jnp.where(mask, 0.5 * (ui - di), ui),
                jnp.where(mask, 0.5 * (ui + di), dr),
                jnp.where(mask, 0.5 * (dr - ur), di),
            )
            real_ref[where_x, up] = new[0]
            imag_ref[where_x, up] = new[1]
            real_ref[where_x, down] = new[2]
            imag_ref[where_x, down] = new[3]
            if group == 0:
                parts = no_mean * new[0] * new[0] + weight * (
                    new[1] * new[1] + new[2] * new[2] + new[3] * new[3]
                )
            else:
                parts = 2.0 * sum(v * v for v in new)
            energy = energy + jnp.sum(parts, 0)
    return energy


def times(value, turn):
    real, imag = value
    eighth = round(8 * turn) % 8
    if abs(8 * turn - round(8 * turn)) > 1e-9:
        cosine, sine = math.cos(2.0 * math.pi * turn), math.sin(2.0 * math.pi * turn)
        return real * cosine - imag * sine, real * sine + imag * cosine
    if eighth % 2:
        half = math.sqrt(0.5)
        real, imag = half * (real - imag), half * (real + imag)
    quarter = eighth // 2
    if quarter == 1:
        return -imag, real
    if quarter == 2:
        return -real, -imag
    if quarter == 3:
        return imag, -real
    return real, imag


def plus(a, b):
    return a[0] + b[0], a[1] + b[1]


def minus(a, b):
    return a[0] - b[0], a[1] - b[1]


def fourier(values, sign):
    count = len(values)
    if count == 1:
        return values
    even, odd = fourier(values[0::2], sign), fourier(values[1::2], sign)
    odd = [times(value, sign * k / count) for k, value in enumerate(odd)]
    return [plus(a, b) for a, b in zip(even, odd)] + [minus(a, b) for a, b in zip(even, odd)]


def x_fourier(values):
    parts = [fourier([values(x + 8 * k) for k in range(4)], -1) for x in range(8)]
    parts = [[times(v, -x * b / WIN) for b, v in enumerate(part)] for x, part in enumerate(parts)]
    for b in range(4):
        yield fourier([parts[x][b] for x in range(8)], -1)


def special_lines(real_0, imag_0, real_16, imag_16):
    lane = lax.broadcasted_iota(jnp.int32, (WIN, LANES), 1) % HALF
    lines = jnp.where(lane == 0, real_0, 0.0)
    for n, line in enumerate((imag_0, real_16, imag_16)):
        lines = jnp.where(lane == n + 1, pltpu.roll(line, n + 1, 1), lines)
    means = jnp.sum(lines, 0, keepdims=True) * (1.0 / WIN)
    lines = jnp.where(lane == 0, lines - means, lines)
    return lines, jnp.sum(jnp.where(lane == 0, lines * lines, 0.0), 0, keepdims=True)


def variance(energy, mean_energy):
    total = jnp.sum(energy, 0, keepdims=True) + mean_energy
    total = jnp.broadcast_to(total, (8, LANES))
    group_row = lax.broadcasted_iota(jnp.int32, (LANES, LANES), 0) // HALF
    group_col = lax.broadcasted_iota(jnp.int32, (LANES, LANES), 1) // HALF
    same = (group_row == group_col).astype(F32)
    summed = jnp.dot(total, same, precision=lax.Precision.HIGHEST, preferred_element_type=F32)
    return summed * (1.0 / (ZS * WIN * WIN * ZS * WIN))


def first_tables(y_ref, z_ref):
    def halves(ref, rows, cols, value):
        high = value.astype(BF16)
        low = (value - high.astype(F32)).astype(BF16)
        for n, part in enumerate((high, low) if cols is None else (high, high, low)):
            if cols is None:
                ref[n * NY : (n + 1) * NY, rows] = part
            else:
                start = n * 2 * LANES
                ref[rows, start + cols.start : start + cols.stop] = part

    row = lax.broadcasted_iota(jnp.int32, (WIN, LANES), 0)
    lane = lax.broadcasted_iota(jnp.int32, (WIN, LANES), 1)
    unit = 2.0 * math.pi / WIN

    frequency = lane % HALF
    turns = (frequency * (row + STEP * (lane // HALF))) % WIN
    cosine = jnp.cos(turns.astype(F32) * unit)
    sine = jnp.where(frequency == 0, 2.0 * (row % 2).astype(F32) - 1.0, jnp.sin(turns.astype(F32) * unit))
    y = lax.broadcasted_iota(jnp.int32, (NY, LANES), 0)
    offset = y - STEP * (lax.broadcasted_iota(jnp.int32, (NY, LANES), 1) // HALF)
    inside = (offset >= 0) & (offset < WIN)
    for n, part in enumerate((cosine, -sine)):
        tall = jnp.concatenate([part] * (NY // WIN), 0)
        halves(y_ref, slice(n * LANES, (n + 1) * LANES), None, jnp.where(inside, tall, 0.0))

    order = jnp.where(row <= HALF, row, WIN + HALF - row)
    turns = (order * (lane % ZS)) % WIN
    cosine, sine = jnp.cos(turns.astype(F32) * unit), jnp.sin(turns.astype(F32) * unit)
    y_lane = lax.broadcasted_iota(jnp.int32, (4 * ZS, LANES), 1)
    same = lax.broadcasted_iota(jnp.int32, (4 * ZS, LANES), 0) // ZS == y_lane // ZS
    blocks = [jnp.where(same, jnp.concatenate([v] * 4, 0), 0.0) for v in (cosine, sine)]
    upper, lower = slice(0, LANES), slice(LANES, 2 * LANES)
    halves(z_ref, upper, upper, blocks[0])
    halves(z_ref, upper, lower, blocks[1])
    halves(z_ref, lower, upper, -blocks[1])
    halves(z_ref, lower, lower, blocks[0])


def first_stage(tile, y_ref, z_ref, real_ref, imag_ref, energy_ref):
    energy = jnp.zeros((8, LANES), F32)
    table = y_ref[...]
    for start in range(0, STEP, 8):
        rows = tile[start : start + 8].reshape(8 * ZS, NY)
        values = dot(jnp.concatenate([rows, rows], 1), table)
        energy = energy + z_stage(
            values[: 4 * ZS], values[4 * ZS :], z_ref, real_ref, imag_ref, start
        )
    energy_ref[...] = energy


def low_kernel(
    tile_ref,
    shift_x_hbm,
    shift_y_hbm,
    real_ref,
    imag_ref,
    energy_ref,
    y_ref,
    z_ref,
    shifts_ref,
    shift_x_ref,
    shift_y_ref,
    sems,
):
    copies = [
        pltpu.make_async_copy(shift_x_hbm, shift_x_ref, sems.at[0]),
        pltpu.make_async_copy(shift_y_hbm, shift_y_ref, sems.at[1]),
    ]
    for copy in copies:
        copy.start()
    first_tables(y_ref, z_ref)
    first_stage(tile_ref[...], y_ref, z_ref, real_ref, imag_ref, energy_ref)
    for copy in copies:
        copy.wait()
    shifts_ref[0:1] = shift_x_ref[...]
    shifts_ref[1:2] = shift_y_ref[...]


def high_kernel(
    next_ref,
    own_ref,
    y_ref,
    z_ref,
    low_real_ref,
    low_imag_ref,
    low_energy_ref,
    real_ref,
    imag_ref,
    lines_ref,
    var_ref,
    high_real_ref,
    high_imag_ref,
    high_energy_ref,
):
    position = lax.axis_index("gx")
    odd = position % 2
    inside = position < lax.axis_size("gx") - 2
    use_next = jnp.where(inside & (odd == 0), 1.0, 0.0).astype(BF16)
    use_own = odd.astype(BF16)
    tile = next_ref[...] * use_next + own_ref[...] * use_own
    first_stage(tile, y_ref, z_ref, high_real_ref, high_imag_ref, high_energy_ref)

    def eight_slots(where_z):
        def value(x):
            if x < STEP:
                return low_real_ref[x, where_z], low_imag_ref[x, where_z]
            return high_real_ref[x - STEP, where_z], high_imag_ref[x - STEP, where_z]

        for b, column in enumerate(x_fourier(value)):
            for a, (real, imag) in enumerate(column):
                real_ref[8 * b + a, where_z] = real
                imag_ref[8 * b + a, where_z] = imag

    for start in range(0, ZS, 8):
        eight_slots(slice(start, start + 8))
    lines = [
        jnp.concatenate([low[:, slot], high[:, slot]], 0)
        for slot in (0, HALF)
        for low, high in ((low_real_ref, high_real_ref), (low_imag_ref, high_imag_ref))
    ]
    lines_ref[...], mean_energy = special_lines(*lines)
    var_ref[...] = variance(low_energy_ref[...] + high_energy_ref[...], mean_energy)


def second_kernel(
    shifts_ref,
    own_ref,
    mate_ref,
    near_own_ref,
    near_mate_ref,
    far_own_ref,
    far_mate_ref,
    mate_near_own_ref,
    mate_near_mate_ref,
    mate_far_own_ref,
    first_real_ref,
    first_imag_ref,
    first_lines_ref,
    first_var_ref,
    y_high_ref,
    y_low_ref,
    z_ref,
    z_inverse_ref,
    y_inverse_ref,
    out_ref,
    region_ref,
    real_ref,
    imag_ref,
    cross_real_ref,
    cross_imag_ref,
    twice_ref,
):
    position = lax.axis_index("gx")
    tiles = lax.axis_size("gx")
    odd = position % 2
    even = 1 - odd
    tiles_below = position - odd - 4
    shifts = shifts_ref[...]
    starts_x = [shifts[0, j] + STEP * (4 + even) for j in range(WY)]
    starts_y = [shifts[1, j] + STEP * j for j in range(WY)]
    tiles_at = (
        (own_ref, 4 + odd),
        (mate_ref, 4 + even),
        (near_own_ref, 3 + 3 * even),
        (near_mate_ref, 2 + 5 * even),
        (far_own_ref, 1 + 7 * even),
        (far_mate_ref, 9 * even),
        (mate_near_own_ref, 3 + 3 * odd),
        (mate_near_mate_ref, 2 + 5 * odd),
        (mate_far_own_ref, 1 + 7 * odd),
    )
    for tile_ref, at in tiles_at:
        region_ref[pl.ds(at * STEP, STEP)] = tile_ref[...]
    for tile in range(10):

        @pl.when((tiles_below + tile < 0) | (tiles_below + tile >= tiles))
        def _(tile=tile):
            region_ref[tile * STEP : (tile + 1) * STEP] = jnp.zeros((STEP, ZS, NY), BF16)

    lane = lax.broadcasted_iota(jnp.int32, (1, LANES), 1)

    def eight_x(start, energy):
        packs = []
        for half in range(2):
            total = None
            for n in range(4):
                j = half * 4 + n
                start_y = starts_y[j]
                block = region_ref[pl.ds(starts_x[j] + start, 8)].reshape(8 * ZS, NY)
                turned = pltpu.roll(block.astype(F32), (n * WIN - start_y) & (LANES - 1), 1)
                y = lane - n * WIN + start_y
                inside = (lane // WIN == n) & (y >= 0) & (y < NY)
                if total is None:
                    total = jnp.where(inside, turned, 0.0)
                else:
                    total = jnp.where(inside, turned, total)
            packs.append(total.astype(BF16))
        windows = jnp.concatenate(packs, 1)
        values = dot(windows, y_high_ref[...]) + dot(windows, y_low_ref[...])
        return energy + z_stage(
            values[: 4 * ZS], values[4 * ZS :], z_ref, real_ref, imag_ref, start
        )

    energy = jnp.zeros((8, LANES), F32)
    for start in range(0, WIN, 8):
        energy = eight_x(start, energy)
    def eight_slots(where_z):
        def value(x):
            return real_ref[x, where_z], imag_ref[x, where_z]

        columns = []
        for b, column in enumerate(x_fourier(value)):
            cross = []
            for a, (gr, gi) in enumerate(column):
                fr, fi = first_real_ref[8 * b + a, where_z], first_imag_ref[8 * b + a, where_z]
                cross.append((fr * gr + fi * gi, fr * gi - fi * gr))
            column = fourier(cross, 1)
            columns.append([times(v, b * s / WIN) for s, v in enumerate(column)])
        for s in range(8):
            u = [column[s] for column in columns]
            even, odd = plus(u[0], u[2]), plus(u[1], u[3])
            here = plus(even, odd)
            even, odd = minus(u[0], u[2]), times(minus(u[1], u[3]), -0.25)
            back = plus(even, odd)
            cross_real_ref[8 + s, where_z], cross_imag_ref[8 + s, where_z] = here
            cross_real_ref[s, where_z], cross_imag_ref[s, where_z] = back

    for start in range(0, ZS, 8):
        eight_slots(slice(start, start + 8))

    lines, mean_energy = special_lines(
        real_ref[:, 0], imag_ref[:, 0], real_ref[:, HALF], imag_ref[:, HALF]
    )
    second_var = variance(energy, mean_energy)
    twice_ref[0:WIN] = lines
    twice_ref[WIN : 2 * WIN] = lines
    first_lines = first_lines_ref[...] * float(WIN)
    sums = []
    for s in range(SR):
        shift = (s - SR // 2) % WIN
        sums.append(
            jnp.sum(first_lines * twice_ref[shift : shift + WIN], 0, keepdims=True)
        )
    sums = jnp.concatenate(sums, 0)
    alone = [sums] + [pltpu.roll(sums, LANES - n, 1) for n in range(1, 4)]
    alone = [v.reshape(SR, 1, LANES) for v in alone]

    rows, zero_lane = positions((4, 8, LANES))
    special = zero_lane & (rows == 0)
    mixed = [zero_lane & (rows != 0), zero_lane]
    scale = 1.0 / (
        WIN**1.5 * (jnp.sqrt(first_var_ref[...] + 1e-6) * jnp.sqrt(second_var + 1e-6))
    )
    pairs = []
    for start in range(0, SR, 8):
        columns = []
        for quarter in range(start, start + 8, 4):
            where_x = slice(quarter, quarter + 4)
            real = [None] * 4
            imag = [None] * 4
            for group in range(2):
                up = slice(group * 8, group * 8 + 8)
                down = slice(group * 8 + 16, group * 8 + 24)
                ur, ui = cross_real_ref[where_x, up], cross_imag_ref[where_x, up]
                dr, di = cross_real_ref[where_x, down], cross_imag_ref[where_x, down]
                mask = mixed[group]
                if group == 0:
                    ur, ui, dr, di = (
                        jnp.where(special, line[where_x], v)
                        for line, v in zip(alone, (ur, ui, dr, di))
                    )
                real[group] = jnp.where(mask, ur - di, ur)
                imag[group] = jnp.where(mask, ui + dr, ui)
                real[group + 2] = jnp.where(mask, ur + di, dr)
                imag[group + 2] = jnp.where(mask, dr - ui, di)
            columns.append(
                jnp.concatenate(
                    [jnp.concatenate(v, 1).reshape(4 * ZS, LANES) for v in (real, imag)], 0
                )
            )
        slots = dot(z_inverse_ref[...], split(jnp.concatenate(columns, 1), 0))
        for h in range(2):
            lanes = slice(h * LANES, (h + 1) * LANES)
            pair = jnp.concatenate([slots[: 4 * SR, lanes], slots[4 * SR :, lanes]], 1)
            pairs.append(pair)
    values = dot(split(jnp.concatenate(pairs, 0), 1), y_inverse_ref[...])
    out_ref[...] = values * scale[0:1]


def product_kernel(made_ref, other_ref, own_ref, out_ref):
    position = lax.axis_index("gx")
    edge = (position == 0) | (position == lax.axis_size("gx") - 1)
    own = own_ref[...]
    lane = lax.broadcasted_iota(jnp.int32, own.shape, 1)
    below = jnp.where(lane < SR, 1.0, pltpu.roll(own, SR, 1))
    above = jnp.where(lane >= LANES - SR, 1.0, pltpu.roll(own, LANES - SR, 1))
    other = jnp.where(edge, 1.0, other_ref[...])
    out_ref[...] = own * made_ref[...] * other * below * above


def params():
    return pltpu.CompilerParams(vmem_limit_bytes=VMEM_LIMIT)


VMEM = pl.BlockSpec(memory_space=pltpu.VMEM)
HBM = pl.BlockSpec(memory_space=pltpu.HBM)


def local(first_volume, second_volume, shift_x, shift_y):
    size = lax.axis_size("gx")
    chips = size // 2

    def send(value, pairs):
        return lax.ppermute(value, "gx", pairs)

    last = size - 1
    mates = [(i, i ^ 1) for i in range(size)]
    near = [(2 * q + 2, 2 * q) for q in range(chips - 1)] + [(last, last - 1)]
    near += [(2 * q - 1, 2 * q + 1) for q in range(1, chips)] + [(0, 1)]
    far = [(2 * q + 4, 2 * q) for q in range(chips - 2)] + [(last, last - 1), (last - 2, last - 3)]
    far += [(2 * q - 3, 2 * q + 1) for q in range(2, chips)] + [(0, 1), (2, 3)]
    near_own = send(second_volume, near)
    mate_tile = send(second_volume, mates)
    far_own = send(second_volume, far)
    near_first = send(first_volume, near)
    mate_first = send(first_volume, mates)
    near_mate = send(mate_tile, near)
    far_mate = send(mate_tile, far)

    half = jax.ShapeDtypeStruct((STEP, ZS, LANES), F32)
    whole = jax.ShapeDtypeStruct((WIN, ZS, LANES), F32)
    lines = jax.ShapeDtypeStruct((WIN, LANES), F32)
    row = jax.ShapeDtypeStruct((8, LANES), F32)
    y_table = jax.ShapeDtypeStruct((2 * NY, 2 * LANES), BF16)
    z_table = jax.ShapeDtypeStruct((2 * LANES, 6 * LANES), BF16)
    shifts = jax.ShapeDtypeStruct((2, WY), shift_x.dtype)

    def first_spectra(kernel, specs, outs, scratch, *operands):
        return pl.pallas_call(
            kernel,
            out_shape=outs,
            in_specs=specs,
            out_specs=(VMEM,) * len(outs),
            scratch_shapes=scratch,
            compiler_params=params(),
            cost_estimate=pl.CostEstimate(
                flops=2 * 10**9, transcendentals=0, bytes_accessed=2 * 10**6
            ),
            name="first_spectra",
        )(*operands)

    *low_part, y_table, z_table, shifts = first_spectra(
        low_kernel,
        [VMEM] + [HBM] * 2,
        (half, half, row, y_table, z_table, shifts),
        [pltpu.VMEM(v.shape, v.dtype) for v in (shift_x, shift_y)]
        + [pltpu.SemaphoreType.DMA((2,))],
        mate_first,
        *(pltpu.with_memory_space_constraint(v, pltpu.HBM) for v in (shift_x, shift_y)),
    )
    near_own, *low_part = lax.optimization_barrier((near_own, *low_part))
    near_first, far_mate = lax.optimization_barrier((near_first, far_mate))
    first_part = first_spectra(
        high_kernel,
        [VMEM] * 7,
        (whole, whole, lines, row),
        [pltpu.VMEM(v.shape, F32) for v in (half, half, row)],
        near_first,
        first_volume,
        y_table,
        z_table,
        *low_part,
    )
    side = (near_own, near_mate, far_own, far_mate)
    mate_side = [send(tile, mates) for tile in side[:3]]

    y_high, y_low = second_y_table()
    maps = pl.pallas_call(
        second_kernel,
        out_shape=jax.ShapeDtypeStruct((SR * SR, LANES), F32),
        in_specs=[VMEM] * 19,
        out_specs=VMEM,
        scratch_shapes=[
            pltpu.VMEM((10 * STEP, ZS, NY), BF16),
            pltpu.VMEM((WIN, ZS, LANES), F32),
            pltpu.VMEM((WIN, ZS, LANES), F32),
            pltpu.VMEM((SR, ZS, LANES), F32),
            pltpu.VMEM((SR, ZS, LANES), F32),
            pltpu.VMEM((2 * WIN, LANES), F32),
        ],
        compiler_params=params(),
        name="second_maps",
    )(
        send(shifts, mates),
        second_volume,
        mate_tile,
        *side,
        *mate_side,
        *first_part,
        y_high,
        y_low,
        z_table,
        z_inverse_table(),
        y_inverse_table(),
    )

    own_maps = send(maps, mates)
    other_maps = send(maps, [(b, a) for a, b in near])
    product = pl.pallas_call(
        product_kernel,
        out_shape=jax.ShapeDtypeStruct((SR * SR, LANES), F32),
        in_specs=[VMEM] * 3,
        out_specs=VMEM,
        compiler_params=params(),
        name="product",
    )(maps, other_maps, own_maps)
    return product.reshape(1, SR, SR, LANES)


def solution(mesh):
    return jax.shard_map(
        local,
        mesh=mesh,
        in_specs=(
            P(("groups", "gx"), None, None),
            P(("groups", "gx"), None, None),
            P(("groups", "gx"), None),
            P(("groups", "gx"), None),
        ),
        out_specs=P(("groups", "gx"), None, None, None),
        check_vma=False,
    )
```

```python
import math

import jax
import jax.numpy as jnp
import numpy as np
from jax import lax
from jax.experimental import pallas as pl
from jax.experimental.pallas import tpu as pltpu
from jax.sharding import PartitionSpec as P

WIN = 32
STEP = 16
ZS = 32
SR = 16
WY = 8
NY = WY * STEP
LANES = 128
HALF = WIN // 2
BF16 = jnp.bfloat16
F32 = jnp.float32
VMEM_LIMIT = 48 * 2**20

Z_ORDER = np.array([*range(16), 16, *range(31, 16, -1)])


def split_table(table):
    high = np.asarray(table, np.float32).astype(BF16)
    low = (np.asarray(table, np.float64) - high.astype(np.float64)).astype(BF16)
    return high, low


def phase(numbers):
    return 2.0 * math.pi * (np.asarray(numbers) % WIN) / WIN


def y_columns():
    angles = phase(np.outer(np.arange(WIN), np.arange(HALF)))
    real, imag = np.cos(angles), -np.sin(angles)
    imag[:, 0] = 1.0 - 2.0 * (np.arange(WIN) % 2)
    return real, imag


def second_y_table():
    real, imag = y_columns()
    table = np.zeros((WY, WIN, 2, WY, HALF))
    for j in range(WY):
        table[j, :, 0, j] = real
        table[j, :, 1, j] = imag
    return split_table(table.reshape(2 * LANES, 2 * LANES))


def three_terms(table, axis):
    high, low = split_table(table)
    return np.concatenate([high, high, low], axis)


def z_inverse_table():
    angles = phase(np.outer(np.arange(SR) - SR // 2, Z_ORDER))
    four = np.eye(4)
    cosine, sine = np.kron(four, np.cos(angles)), np.kron(four, np.sin(angles))
    return three_terms(np.block([[cosine, -sine], [sine, cosine]]), 1)


def y_inverse_table():
    shifts = np.arange(SR) - SR // 2
    angles = phase(np.outer(np.arange(HALF), shifts))
    real, imag = 2.0 * np.cos(angles), -2.0 * np.sin(angles)
    real[0] = 1.0
    imag[0] = 1.0 - 2.0 * (shifts % 2)
    eight = np.eye(WY)
    table = np.concatenate([np.kron(eight, real), np.kron(eight, imag)], 0)
    return three_terms(table / WIN**3, 0)


def dot(a, b):
    return jnp.dot(a, b, preferred_element_type=F32)


def split(value, axis):
    high = value.astype(BF16)
    low = (value - high.astype(F32)).astype(BF16)
    return jnp.concatenate([high, low, high], axis)


def positions(shape):
    rows = lax.broadcasted_iota(jnp.int32, shape, len(shape) - 2)
    lanes = lax.broadcasted_iota(jnp.int32, shape, len(shape) - 1)
    return rows, lanes % HALF == 0


def z_stage(part_0, part_1, table_ref, real_ref, imag_ref, start):
    columns = [
        jnp.concatenate([part[:, :LANES], part[:, LANES:]], 0) for part in (part_0, part_1)
    ]
    slots = dot(table_ref[...], split(jnp.concatenate(columns, 1), 0))
    rows, zero_lane = positions((4, 8, LANES))
    mixed = [zero_lane & (rows != 0), zero_lane]
    weight = jnp.where(zero_lane & (rows == 0), 1.0, 2.0)
    no_mean = jnp.where(zero_lane & (rows == 0), 0.0, 2.0)
    energy = jnp.zeros((8, LANES), F32)
    for h in range(2):
        lanes = slice(h * LANES, (h + 1) * LANES)
        real = slots[: 4 * ZS, lanes].reshape(4, ZS, LANES)
        imag = slots[4 * ZS :, lanes].reshape(4, ZS, LANES)
        where_x = pl.ds(start + 4 * h, 4)
        for group in range(2):
            up = slice(group * 8, group * 8 + 8)
            down = slice(group * 8 + 16, group * 8 + 24)
            ur, ui, dr, di = real[:, up], imag[:, up], real[:, down], imag[:, down]
            mask = mixed[group]
            new = (
                jnp.where(mask, 0.5 * (ur + dr), ur),
                jnp.where(mask, 0.5 * (ui - di), ui),
                jnp.where(mask, 0.5 * (ui + di), dr),
                jnp.where(mask, 0.5 * (dr - ur), di),
            )
            real_ref[where_x, up] = new[0]
            imag_ref[where_x, up] = new[1]
            real_ref[where_x, down] = new[2]
            imag_ref[where_x, down] = new[3]
            if group == 0:
                parts = no_mean * new[0] * new[0] + weight * (
                    new[1] * new[1] + new[2] * new[2] + new[3] * new[3]
                )
            else:
                parts = 2.0 * sum(v * v for v in new)
            energy = energy + jnp.sum(parts, 0)
    return energy


def times(value, turn):
    real, imag = value
    eighth = round(8 * turn) % 8
    if abs(8 * turn - round(8 * turn)) > 1e-9:
        cosine, sine = math.cos(2.0 * math.pi * turn), math.sin(2.0 * math.pi * turn)
        return real * cosine - imag * sine, real * sine + imag * cosine
    if eighth % 2:
        half = math.sqrt(0.5)
        real, imag = half * (real - imag), half * (real + imag)
    quarter = eighth // 2
    if quarter == 1:
        return -imag, real
    if quarter == 2:
        return -real, -imag
    if quarter == 3:
        return imag, -real
    return real, imag


def plus(a, b):
    return a[0] + b[0], a[1] + b[1]


def minus(a, b):
    return a[0] - b[0], a[1] - b[1]


def fourier(values, sign):
    count = len(values)
    if count == 1:
        return values
    even, odd = fourier(values[0::2], sign), fourier(values[1::2], sign)
    odd = [times(value, sign * k / count) for k, value in enumerate(odd)]
    return [plus(a, b) for a, b in zip(even, odd)] + [minus(a, b) for a, b in zip(even, odd)]


def x_fourier(values):
    parts = [fourier([values(x + 8 * k) for k in range(4)], -1) for x in range(8)]
    parts = [[times(v, -x * b / WIN) for b, v in enumerate(part)] for x, part in enumerate(parts)]
    for b in range(4):
        yield fourier([parts[x][b] for x in range(8)], -1)


def special_lines(real_0, imag_0, real_16, imag_16):
    lane = lax.broadcasted_iota(jnp.int32, (WIN, LANES), 1) % HALF
    lines = jnp.where(lane == 0, real_0, 0.0)
    for n, line in enumerate((imag_0, real_16, imag_16)):
        lines = jnp.where(lane == n + 1, pltpu.roll(line, n + 1, 1), lines)
    means = jnp.sum(lines, 0, keepdims=True) * (1.0 / WIN)
    lines = jnp.where(lane == 0, lines - means, lines)
    return lines, jnp.sum(jnp.where(lane == 0, lines * lines, 0.0), 0, keepdims=True)


def variance(energy, mean_energy):
    total = jnp.sum(energy, 0, keepdims=True) + mean_energy
    total = jnp.broadcast_to(total, (8, LANES))
    place = lax.broadcasted_iota(jnp.int32, (8, LANES), 1) % HALF
    for step in (1, 2, 4, 8):
        ahead = pltpu.roll(total, step, 1)
        around = pltpu.roll(total, LANES - HALF + step, 1)
        total = total + jnp.where(place >= step, ahead, around)
    return total * (1.0 / (ZS * WIN * WIN * ZS * WIN))


def first_tables(y_ref, z_ref):
    def halves(ref, rows, cols, value):
        high = value.astype(BF16)
        low = (value - high.astype(F32)).astype(BF16)
        for n, part in enumerate((high, low) if cols is None else (high, high, low)):
            if cols is None:
                ref[n * NY : (n + 1) * NY, rows] = part
            else:
                start = n * 2 * LANES
                ref[rows, start + cols.start : start + cols.stop] = part

    row = lax.broadcasted_iota(jnp.int32, (WIN, LANES), 0)
    lane = lax.broadcasted_iota(jnp.int32, (WIN, LANES), 1)
    unit = 2.0 * math.pi / WIN

    frequency = lane % HALF
    turns = (frequency * (row + STEP * (lane // HALF))) % WIN
    cosine = jnp.cos(turns.astype(F32) * unit)
    sine = jnp.where(frequency == 0, 2.0 * (row % 2).astype(F32) - 1.0, jnp.sin(turns.astype(F32) * unit))
    y = lax.broadcasted_iota(jnp.int32, (NY, LANES), 0)
    offset = y - STEP * (lax.broadcasted_iota(jnp.int32, (NY, LANES), 1) // HALF)
    inside = (offset >= 0) & (offset < WIN)
    for n, part in enumerate((cosine, -sine)):
        tall = jnp.concatenate([part] * (NY // WIN), 0)
        halves(y_ref, slice(n * LANES, (n + 1) * LANES), None, jnp.where(inside, tall, 0.0))

    order = jnp.where(row <= HALF, row, WIN + HALF - row)
    turns = (order * (lane % ZS)) % WIN
    cosine, sine = jnp.cos(turns.astype(F32) * unit), jnp.sin(turns.astype(F32) * unit)
    y_lane = lax.broadcasted_iota(jnp.int32, (4 * ZS, LANES), 1)
    same = lax.broadcasted_iota(jnp.int32, (4 * ZS, LANES), 0) // ZS == y_lane // ZS
    blocks = [jnp.where(same, jnp.concatenate([v] * 4, 0), 0.0) for v in (cosine, sine)]
    upper, lower = slice(0, LANES), slice(LANES, 2 * LANES)
    halves(z_ref, upper, upper, blocks[0])
    halves(z_ref, upper, lower, blocks[1])
    halves(z_ref, lower, upper, -blocks[1])
    halves(z_ref, lower, lower, blocks[0])


def first_stage(tile, y_ref, z_ref, real_ref, imag_ref, energy_ref):
    energy = jnp.zeros((8, LANES), F32)
    table = y_ref[...]
    for start in range(0, STEP, 8):
        rows = tile[start : start + 8].reshape(8 * ZS, NY)
        values = dot(jnp.concatenate([rows, rows], 1), table)
        energy = energy + z_stage(
            values[: 4 * ZS], values[4 * ZS :], z_ref, real_ref, imag_ref, start
        )
    energy_ref[...] = energy


def low_kernel(
    tile_ref,
    shift_x_hbm,
    shift_y_hbm,
    real_ref,
    imag_ref,
    energy_ref,
    y_ref,
    z_ref,
    shifts_ref,
    shift_x_ref,
    shift_y_ref,
    sems,
):
    copies = [
        pltpu.make_async_copy(shift_x_hbm, shift_x_ref, sems.at[0]),
        pltpu.make_async_copy(shift_y_hbm, shift_y_ref, sems.at[1]),
    ]
    for copy in copies:
        copy.start()
    first_tables(y_ref, z_ref)
    first_stage(tile_ref[...], y_ref, z_ref, real_ref, imag_ref, energy_ref)
    for copy in copies:
        copy.wait()
    shifts_ref[0:1] = shift_x_ref[...]
    shifts_ref[1:2] = shift_y_ref[...]


def high_kernel(
    next_ref,
    own_ref,
    y_ref,
    z_ref,
    low_real_ref,
    low_imag_ref,
    low_energy_ref,
    real_ref,
    imag_ref,
    lines_ref,
    var_ref,
    high_real_ref,
    high_imag_ref,
    high_energy_ref,
):
    position = lax.axis_index("gx")
    odd = position % 2
    inside = position < lax.axis_size("gx") - 2
    use_next = jnp.where(inside & (odd == 0), 1.0, 0.0).astype(BF16)
    use_own = odd.astype(BF16)
    tile = next_ref[...] * use_next + own_ref[...] * use_own
    first_stage(tile, y_ref, z_ref, high_real_ref, high_imag_ref, high_energy_ref)

    def eight_slots(where_z):
        def value(x):
            if x < STEP:
                return low_real_ref[x, where_z], low_imag_ref[x, where_z]
            return high_real_ref[x - STEP, where_z], high_imag_ref[x - STEP, where_z]

        for b, column in enumerate(x_fourier(value)):
            for a, (real, imag) in enumerate(column):
                real_ref[8 * b + a, where_z] = real
                imag_ref[8 * b + a, where_z] = imag

    for start in range(0, ZS, 8):
        eight_slots(slice(start, start + 8))
    lines = [
        jnp.concatenate([low[:, slot], high[:, slot]], 0)
        for slot in (0, HALF)
        for low, high in ((low_real_ref, high_real_ref), (low_imag_ref, high_imag_ref))
    ]
    lines_ref[...], mean_energy = special_lines(*lines)
    var_ref[...] = variance(low_energy_ref[...] + high_energy_ref[...], mean_energy)


def second_kernel(
    shifts_ref,
    own_ref,
    mate_ref,
    near_own_ref,
    near_mate_ref,
    far_own_ref,
    far_mate_ref,
    mate_near_own_ref,
    mate_near_mate_ref,
    mate_far_own_ref,
    first_real_ref,
    first_imag_ref,
    first_lines_ref,
    first_var_ref,
    y_high_ref,
    y_low_ref,
    z_ref,
    z_inverse_ref,
    y_inverse_ref,
    out_ref,
    region_ref,
    real_ref,
    imag_ref,
    cross_real_ref,
    cross_imag_ref,
    twice_ref,
):
    position = lax.axis_index("gx")
    tiles = lax.axis_size("gx")
    odd = position % 2
    even = 1 - odd
    tiles_below = position - odd - 4
    shifts = shifts_ref[...]
    starts_x = [shifts[0, j] + STEP * (4 + even) for j in range(WY)]
    starts_y = [shifts[1, j] + STEP * j for j in range(WY)]
    tiles_at = (
        (own_ref, 4 + odd),
        (mate_ref, 4 + even),
        (near_own_ref, 3 + 3 * even),
        (near_mate_ref, 2 + 5 * even),
        (far_own_ref, 1 + 7 * even),
        (far_mate_ref, 9 * even),
        (mate_near_own_ref, 3 + 3 * odd),
        (mate_near_mate_ref, 2 + 5 * odd),
        (mate_far_own_ref, 1 + 7 * odd),
    )
    for tile_ref, at in tiles_at:
        region_ref[pl.ds(at * STEP, STEP)] = tile_ref[...]
    for tile in range(10):

        @pl.when((tiles_below + tile < 0) | (tiles_below + tile >= tiles))
        def _(tile=tile):
            region_ref[tile * STEP : (tile + 1) * STEP] = jnp.zeros((STEP, ZS, NY), BF16)

    lane = lax.broadcasted_iota(jnp.int32, (1, LANES), 1)

    def eight_x(start):
        packs = []
        for half in range(2):
            total = None
            for n in range(4):
                j = half * 4 + n
                start_y = starts_y[j]
                block = region_ref[pl.ds(starts_x[j] + start, 8)].reshape(8 * ZS, NY)
                turned = pltpu.roll(block.astype(F32), (n * WIN - start_y) & (LANES - 1), 1)
                y = lane - n * WIN + start_y
                inside = (lane // WIN == n) & (y >= 0) & (y < NY)
                if total is None:
                    total = jnp.where(inside, turned, 0.0)
                else:
                    total = jnp.where(inside, turned, total)
            packs.append(total.astype(BF16))
        return jnp.concatenate(packs, 1)

    energy = jnp.zeros((8, LANES), F32)
    for base in range(0, WIN, 16):
        windows = jnp.concatenate([eight_x(base + x) for x in range(0, 16, 8)], 0)
        values = dot(windows, y_high_ref[...]) + dot(windows, y_low_ref[...])
        for x in range(0, 16, 8):
            part = values[x * ZS : (x + 8) * ZS]
            energy = energy + z_stage(
                part[: 4 * ZS], part[4 * ZS :], z_ref, real_ref, imag_ref, base + x
            )
    def eight_slots(where_z):
        def value(x):
            return real_ref[x, where_z], imag_ref[x, where_z]

        columns = []
        for b, column in enumerate(x_fourier(value)):
            cross = []
            for a, (gr, gi) in enumerate(column):
                fr, fi = first_real_ref[8 * b + a, where_z], first_imag_ref[8 * b + a, where_z]
                cross.append((fr * gr + fi * gi, fr * gi - fi * gr))
            column = fourier(cross, 1)
            columns.append([times(v, b * s / WIN) for s, v in enumerate(column)])
        for s in range(8):
            u = [column[s] for column in columns]
            even, odd = plus(u[0], u[2]), plus(u[1], u[3])
            here = plus(even, odd)
            even, odd = minus(u[0], u[2]), times(minus(u[1], u[3]), -0.25)
            back = plus(even, odd)
            cross_real_ref[8 + s, where_z], cross_imag_ref[8 + s, where_z] = here
            cross_real_ref[s, where_z], cross_imag_ref[s, where_z] = back

    for start in range(0, ZS, 8):
        eight_slots(slice(start, start + 8))

    lines, mean_energy = special_lines(
        real_ref[:, 0], imag_ref[:, 0], real_ref[:, HALF], imag_ref[:, HALF]
    )
    second_var = variance(energy, mean_energy)
    twice_ref[0:WIN] = lines
    twice_ref[WIN : 2 * WIN] = lines
    first_lines = first_lines_ref[...] * float(WIN)
    sums = []
    for s in range(SR):
        shift = (s - SR // 2) % WIN
        sums.append(
            jnp.sum(first_lines * twice_ref[shift : shift + WIN], 0, keepdims=True)
        )
    sums = jnp.concatenate(sums, 0)
    alone = [sums] + [pltpu.roll(sums, LANES - n, 1) for n in range(1, 4)]
    alone = [v.reshape(SR, 1, LANES) for v in alone]

    rows, zero_lane = positions((4, 8, LANES))
    special = zero_lane & (rows == 0)
    mixed = [zero_lane & (rows != 0), zero_lane]
    scale = 1.0 / (
        WIN**1.5 * (jnp.sqrt(first_var_ref[...] + 1e-6) * jnp.sqrt(second_var + 1e-6))
    )
    pairs = []
    for start in range(0, SR, 8):
        columns = []
        for quarter in range(start, start + 8, 4):
            where_x = slice(quarter, quarter + 4)
            real = [None] * 4
            imag = [None] * 4
            for group in range(2):
                up = slice(group * 8, group * 8 + 8)
                down = slice(group * 8 + 16, group * 8 + 24)
                ur, ui = cross_real_ref[where_x, up], cross_imag_ref[where_x, up]
                dr, di = cross_real_ref[where_x, down], cross_imag_ref[where_x, down]
                mask = mixed[group]
                if group == 0:
                    ur, ui, dr, di = (
                        jnp.where(special, line[where_x], v)
                        for line, v in zip(alone, (ur, ui, dr, di))
                    )
                real[group] = jnp.where(mask, ur - di, ur)
                imag[group] = jnp.where(mask, ui + dr, ui)
                real[group + 2] = jnp.where(mask, ur + di, dr)
                imag[group + 2] = jnp.where(mask, dr - ui, di)
            columns.append(
                jnp.concatenate(
                    [jnp.concatenate(v, 1).reshape(4 * ZS, LANES) for v in (real, imag)], 0
                )
            )
        slots = dot(z_inverse_ref[...], split(jnp.concatenate(columns, 1), 0))
        for h in range(2):
            lanes = slice(h * LANES, (h + 1) * LANES)
            pair = jnp.concatenate([slots[: 4 * SR, lanes], slots[4 * SR :, lanes]], 1)
            pairs.append(pair)
    values = dot(split(jnp.concatenate(pairs, 0), 1), y_inverse_ref[...])
    out_ref[...] = values * scale[0:1]


def product_kernel(made_ref, other_ref, own_ref, out_ref):
    position = lax.axis_index("gx")
    edge = (position == 0) | (position == lax.axis_size("gx") - 1)
    own = own_ref[...]
    lane = lax.broadcasted_iota(jnp.int32, own.shape, 1)
    below = jnp.where(lane < SR, 1.0, pltpu.roll(own, SR, 1))
    above = jnp.where(lane >= LANES - SR, 1.0, pltpu.roll(own, LANES - SR, 1))
    other = jnp.where(edge, 1.0, other_ref[...])
    out_ref[...] = own * made_ref[...] * other * below * above


def params():
    return pltpu.CompilerParams(vmem_limit_bytes=VMEM_LIMIT)


VMEM = pl.BlockSpec(memory_space=pltpu.VMEM)
HBM = pl.BlockSpec(memory_space=pltpu.HBM)


def local(first_volume, second_volume, shift_x, shift_y):
    size = lax.axis_size("gx")
    chips = size // 2

    def send(value, pairs):
        return lax.ppermute(value, "gx", pairs)

    last = size - 1
    mates = [(i, i ^ 1) for i in range(size)]
    near = [(2 * q + 2, 2 * q) for q in range(chips - 1)] + [(last, last - 1)]
    near += [(2 * q - 1, 2 * q + 1) for q in range(1, chips)] + [(0, 1)]
    far = [(2 * q + 4, 2 * q) for q in range(chips - 2)] + [(last, last - 1), (last - 2, last - 3)]
    far += [(2 * q - 3, 2 * q + 1) for q in range(2, chips)] + [(0, 1), (2, 3)]
    near_own = send(second_volume, near)
    mate_tile = send(second_volume, mates)
    far_own = send(second_volume, far)
    near_first = send(first_volume, near)
    mate_first = send(first_volume, mates)
    near_mate = send(mate_tile, near)
    far_mate = send(mate_tile, far)

    half = jax.ShapeDtypeStruct((STEP, ZS, LANES), F32)
    whole = jax.ShapeDtypeStruct((WIN, ZS, LANES), F32)
    lines = jax.ShapeDtypeStruct((WIN, LANES), F32)
    row = jax.ShapeDtypeStruct((8, LANES), F32)
    y_table = jax.ShapeDtypeStruct((2 * NY, 2 * LANES), BF16)
    z_table = jax.ShapeDtypeStruct((2 * LANES, 6 * LANES), BF16)
    shifts = jax.ShapeDtypeStruct((2, WY), shift_x.dtype)

    def first_spectra(kernel, specs, outs, scratch, *operands):
        return pl.pallas_call(
            kernel,
            out_shape=outs,
            in_specs=specs,
            out_specs=(VMEM,) * len(outs),
            scratch_shapes=scratch,
            compiler_params=params(),
            cost_estimate=pl.CostEstimate(
                flops=2 * 10**9, transcendentals=0, bytes_accessed=2 * 10**6
            ),
            name="first_spectra",
        )(*operands)

    *low_part, y_table, z_table, shifts = first_spectra(
        low_kernel,
        [VMEM] + [HBM] * 2,
        (half, half, row, y_table, z_table, shifts),
        [pltpu.VMEM(v.shape, v.dtype) for v in (shift_x, shift_y)]
        + [pltpu.SemaphoreType.DMA((2,))],
        mate_first,
        *(pltpu.with_memory_space_constraint(v, pltpu.HBM) for v in (shift_x, shift_y)),
    )
    near_own, *low_part = lax.optimization_barrier((near_own, *low_part))
    near_first, far_mate = lax.optimization_barrier((near_first, far_mate))
    first_part = first_spectra(
        high_kernel,
        [VMEM] * 7,
        (whole, whole, lines, row),
        [pltpu.VMEM(v.shape, F32) for v in (half, half, row)],
        near_first,
        first_volume,
        y_table,
        z_table,
        *low_part,
    )
    side = (near_own, near_mate, far_own, far_mate)
    mate_side = [send(tile, mates) for tile in side[:3]]

    y_high, y_low = second_y_table()
    maps = pl.pallas_call(
        second_kernel,
        out_shape=jax.ShapeDtypeStruct((SR * SR, LANES), F32),
        in_specs=[VMEM] * 19,
        out_specs=VMEM,
        scratch_shapes=[
            pltpu.VMEM((10 * STEP, ZS, NY), BF16),
            pltpu.VMEM((WIN, ZS, LANES), F32),
            pltpu.VMEM((WIN, ZS, LANES), F32),
            pltpu.VMEM((SR, ZS, LANES), F32),
            pltpu.VMEM((SR, ZS, LANES), F32),
            pltpu.VMEM((2 * WIN, LANES), F32),
        ],
        compiler_params=params(),
        name="second_maps",
    )(
        send(shifts, mates),
        second_volume,
        mate_tile,
        *side,
        *mate_side,
        *first_part,
        y_high,
        y_low,
        z_table,
        z_inverse_table(),
        y_inverse_table(),
    )

    own_maps = send(maps, mates)
    other_maps = send(maps, [(b, a) for a, b in near])
    product = pl.pallas_call(
        product_kernel,
        out_shape=jax.ShapeDtypeStruct((SR * SR, LANES), F32),
        in_specs=[VMEM] * 3,
        out_specs=VMEM,
        compiler_params=params(),
        name="product",
    )(maps, other_maps, own_maps)
    return product.reshape(1, SR, SR, LANES)


def solution(mesh):
    return jax.shard_map(
        local,
        mesh=mesh,
        in_specs=(
            P(("groups", "gx"), None, None),
            P(("groups", "gx"), None, None),
            P(("groups", "gx"), None),
            P(("groups", "gx"), None),
        ),
        out_specs=P(("groups", "gx"), None, None, None),
        check_vma=False,
    )
```
